128 devices in a mesh: gz: 16 (over y_lo, z, core), ta: 8 (over y_hi, x).
Axes of the slice: x: 4, y: 4 (y_hi: 2, y_lo: 2; y = y_hi * 2 + y_lo), z: 4, core: 2. Of those that a mesh axis runs over, the one named last changes fastest.
Arguments:
- charge: float32 [1024, 128, 128], P('gz', 'ta'), may hold values from -6 to 6
- green_hat: float32 [256, 256, 2048], P(None, 'ta', 'gz'), may hold values from 0.5 to 5
Outputs:
- potential: float32 [1024, 128, 128], P('gz', 'ta')
The draws below stay inside these ranges and needn't reach their ends.
All inputs are finite; a program needn't handle non-finite values.
Results may differ from the reference program's by a relative error of at most 0.00007.
Values sent between devices are 32-bit elements; how exact they have to be, the bound alone decides.
A program may use at most 64 MiB of HBM per device.

```python
import math
import jax
import jax.numpy as jnp
import numpy as np
from jax import lax

GRID_T = 256
GRID_Z = 2048
PHYS_T = 128
PHYS_Z = 1024
SLAB_LEN = 64
RESIDUES = 32
ZBITS = 4


def draw_charge(key, part):
    shape = (PHYS_Z, PHYS_T, PHYS_T)
    return jnp.clip(jax.random.normal(key, shape, jnp.float32), -6.0, 6.0)


def shard_levels(own_key, extent, cuts, low, largest):
    loudness, own = 1.0, jax.random.fold_in(own_key, 6)
    for dim, shards_of in cuts:
        heights = jnp.exp(jax.random.uniform(jax.random.fold_in(own, dim), (shards_of,), jnp.float32, low / len(cuts), largest / len(cuts)))
        loudness = loudness * jnp.repeat(heights, extent[dim] // shards_of).reshape([-1 if axis == dim else 1 for axis in range(len(extent))])
    return loudness


def setup_inputs(seed: int = 0) -> dict:
    seeds = jax.random.split(jax.random.key(seed), 3)
    charge = draw_charge(jax.random.fold_in(seeds[2], 71), 0)
    green_hat = jnp.clip(jnp.exp(math.log(5.0) - 2.3025851 * jax.random.uniform(seeds[1], (GRID_T, GRID_T, GRID_Z), jnp.float32) ** shard_levels(seeds[1], (GRID_T, GRID_T, GRID_Z), ((1, 8), (2, 16)), -0.2, 0.2)), 0.5, 5.0)
    return {"charge": charge, "green_hat": green_hat}


def slot_index():
    wavenum = np.arange(GRID_Z)
    multiple = wavenum // RESIDUES
    residue = wavenum % RESIDUES
    source = residue // 2
    flipped = source * 0
    for bit_index in range(ZBITS):
        flipped = flipped + ((source >> bit_index) & 1) * (1 << (ZBITS - 1 - bit_index))
    return (flipped * 2 * SLAB_LEN + (residue % 2) * SLAB_LEN + multiple).astype(np.int32)


def reference(charge, green_hat):
    slots = jnp.asarray(slot_index()).astype(jnp.int32)
    kernel = jnp.transpose(jnp.take(green_hat, slots, axis=2), (2, 0, 1))
    padded = jnp.pad(charge, ((0, GRID_Z - PHYS_Z), (0, 0), (0, 0)))
    along_z = jnp.fft.fft(padded, axis=0)
    block_count = max(GRID_Z // 256, 1)
    block_len = GRID_Z // block_count

    def solve_block(pieces):
        spec_part, kernel_part = pieces
        full_part = jnp.fft.fft2(spec_part, s=(GRID_T, GRID_T), axes=(1, 2))
        inverted = jnp.fft.ifft2(full_part * kernel_part, axes=(1, 2))
        return inverted[:, :PHYS_T, :PHYS_T]

    blended = lax.map(solve_block, (along_z.reshape(block_count, block_len, PHYS_T, PHYS_T),
                                    kernel.reshape(block_count, block_len, GRID_T, GRID_T)))
    blended = blended.reshape(GRID_Z, PHYS_T, PHYS_T)
    result = jnp.fft.ifft(blended, axis=0)[:PHYS_Z]
    return jnp.real(result).astype(jnp.float32)
```

```python
import math

import jax
import jax.numpy as jnp
from jax import lax
from jax.sharding import PartitionSpec as P

FULL_PRECISION = lax.Precision.HIGH


def turns(product, modulus):
    return 2.0 * math.pi / modulus * (product % modulus).astype(jnp.float32)


def phase_table(phase):
    cosine = jnp.cos(phase)
    sine_part = jnp.sin(phase)
    upper_row = jnp.stack([cosine, sine_part], axis=1)
    lower_row = jnp.stack([-sine_part, cosine], axis=1)
    return jnp.stack([upper_row, lower_row], axis=0)


def reversed_bits(number, bit_count):
    flipped = jnp.zeros_like(number)
    for bit_index in range(bit_count):
        flipped = flipped + (number >> bit_index & 1) * (1 << bit_count - 1 - bit_index)
    return flipped


def on_device(charge, green_hat):
    slab_count = lax.axis_size("gz")
    bit_count = slab_count.bit_length() - 1
    slab_rank = lax.axis_index("gz")
    slab_len, width_x, phys_t = charge.shape
    grid_t = 2 * phys_t
    grid_z = 2 * slab_len * slab_count
    kz_dev = 2 * slab_len
    residues = 2 * slab_count
    rank_rev = reversed_bits(slab_rank, bit_count)
    part = slab_len // slab_count
    slabs = jnp.arange(slab_count, dtype=jnp.int32)
    residue = (2 * reversed_bits(slabs, bit_count)[:, None] + jnp.arange(2, dtype=jnp.int32)).reshape(-1)
    slab_phase = turns(slabs[:, None] * residue[None, :], residues)
    to_residue = jnp.stack([jnp.cos(slab_phase), -jnp.sin(slab_phase)], axis=1)
    to_residue = to_residue.reshape(slab_count, 2, slab_count, 2)
    gathered = lax.all_to_all(
        charge.reshape(slab_count, part, width_x, phys_t), "gz", split_axis=0, concat_axis=0, tiled=True
    )
    partial = jnp.einsum("gwxy,gcre->rcewxy", gathered, to_residue, precision=FULL_PRECISION)
    exchanged = lax.all_to_all(partial, "gz", split_axis=0, concat_axis=0, tiled=True)
    series = exchanged.transpose(1, 2, 0, 3, 4, 5).reshape(2, 2, slab_len, width_x, phys_t)
    flat_index = jnp.arange(kz_dev, dtype=jnp.int32)
    half_id = flat_index // slab_len
    inner_pos = flat_index % slab_len
    wavenum = residues * inner_pos + 2 * rank_rev + half_id
    same_half = (half_id[:, None] == half_id[None, :]).astype(jnp.float32)
    forward_z = (
        phase_table(-turns(inner_pos[:, None] * wavenum[None, :], grid_z))
        * same_half[None, :, None, :]
    )
    spectrum = jnp.einsum(
        "cwxy,cwdk->dkxy",
        series.reshape(2, kz_dev, width_x, phys_t),
        forward_z,
        precision=FULL_PRECISION,
    )
    cells = jnp.arange(phys_t, dtype=jnp.int32)
    freqs = jnp.arange(grid_t, dtype=jnp.int32)
    forward_t = phase_table(-turns(cells[:, None] * freqs[None, :], grid_t))
    inverse_t = phase_table(turns(freqs[:, None] * cells[None, :], grid_t))
    planes = jnp.einsum("czxy,cydk->dxkz", spectrum, forward_t, precision=FULL_PRECISION)
    pencils = lax.all_to_all(planes, "ta", split_axis=2, concat_axis=1, tiled=True)
    full_field = jnp.einsum("cxyz,cxdk->dkyz", pencils, forward_t, precision=FULL_PRECISION)
    scale = 1.0 / (grid_t * grid_t * grid_z)
    weighted = full_field * (green_hat * scale)[None]
    inverted = jnp.einsum("ckyz,ckdx->dxyz", weighted, inverse_t, precision=FULL_PRECISION)
    planes_back = lax.all_to_all(inverted, "ta", split_axis=1, concat_axis=2, tiled=True)
    along_y = jnp.einsum("cxkz,ckdy->dzxy", planes_back, inverse_t, precision=FULL_PRECISION)
    inverse_z = (
        phase_table(turns(wavenum[:, None] * inner_pos[None, :], grid_z))
        * same_half[None, :, None, :]
    )
    series = jnp.einsum("czxy,czdw->dwxy", along_y, inverse_z, precision=FULL_PRECISION)
    series = series.reshape(2, 2, slab_count, part, width_x, phys_t).transpose(2, 0, 1, 3, 4, 5)
    returned = lax.all_to_all(series, "gz", split_axis=0, concat_axis=0, tiled=True)
    summed = jnp.einsum("rcewxy,gcre->gwxy", returned, to_residue, precision=FULL_PRECISION)
    result = lax.all_to_all(summed, "gz", split_axis=0, concat_axis=0, tiled=True)
    return result.reshape(slab_len, width_x, phys_t)


def solution(mesh):
    in_specs = (P("gz", "ta", None), P(None, "ta", "gz"))
    out_specs = P("gz", "ta", None)
    return jax.shard_map(
        on_device, mesh=mesh, in_specs=in_specs, out_specs=out_specs, check_vma=False
    )
```

```python
import functools

import jax
import jax.numpy as jnp
import ml_dtypes
import numpy as np
from jax import lax
from jax.experimental import pallas as pl
from jax.experimental.pallas import tpu as pltpu
from jax.sharding import PartitionSpec as P

MESH = pl.DeviceIdType.MESH
F32 = jnp.float32
BF16 = jnp.bfloat16
CHUNKS = 4
KY = 32
KY_STEP = KY // CHUNKS


def halves(table):
    high = table.astype(ml_dtypes.bfloat16)
    low = (table - high.astype(np.float64)).astype(ml_dtypes.bfloat16)
    return np.stack([high, low])


def tables():
    peer = np.arange(32)
    own = np.arange(4)
    x_of = (own[None] // 2) * 64 + (peer[:, None] // 8) * 16 + (peer[:, None] % 8) * 2 + own[None] % 2
    kx = np.arange(256)
    angle = 2 * np.pi / 256 * (kx[:, None, None] * x_of[None] % 256)
    cosine, sine = np.cos(angle), np.sin(angle)
    wx = np.stack([np.stack([cosine, sine], 2), np.stack([-sine, cosine], 2)]).reshape(512, 256)
    y = np.arange(128)
    wy = []
    for y_half in range(2):
        ky = 128 * y_half + np.arange(128)
        angle = 2 * np.pi / 256 * (ky[:, None] * y[None] % 256)
        cosine, sine = np.cos(angle), np.sin(angle)
        wy.append(np.block([[cosine, sine], [-sine, cosine]]))
    wy = np.stack(wy)
    v = np.arange(128)
    low_bits = np.concatenate([2 * np.arange(64), 2 * np.arange(64) + 1])
    angle = 2 * np.pi / 128 * (low_bits[:, None] * v[None] % 128)
    alpha = np.stack([np.cos(angle), np.sin(angle)]).astype(np.float32)
    reverse = np.array([0, 2, 1, 3])
    s = 4 * reverse[None, :, None] + 2 * np.arange(2)[:, None, None] + np.arange(2)[None, None]
    angle = 2 * np.pi / 2048 * (s.reshape(2, 8)[..., None] * v % 2048)
    beta = np.stack([np.cos(angle), np.sin(angle)], 2).astype(np.float32)
    beta = np.pad(beta, ((0, 0), (0, 0), (0, 6), (0, 0)))
    return (
        halves(wx),
        halves(wx.T * 2.0**-27),
        np.stack([halves(w) for w in wy]),
        np.stack([halves(w.T) for w in wy]),
        alpha,
        beta,
    )


def split(value):
    high = value.astype(BF16)
    return high, (value - high.astype(F32)).astype(BF16)


def weight3(high, low):
    return jnp.concatenate([high, high, low], axis=1)


def data3(value, axis):
    high, low = split(value)
    return jnp.concatenate([high, low, high], axis=axis)


def dot_nn(weight, data):
    return jnp.dot(weight, data, preferred_element_type=F32)


def dot_nt(weight, data):
    return lax.dot_general(weight, data, (((1,), (1,)), ((), ())), preferred_element_type=F32)


def kernel(
    charge, green, wx_hbm, wxi_hbm, wy_hbm, wyi_hbm, alpha_hbm, beta_hbm,
    out,
    g, wx, wxi, wy, wyi, alpha, beta, wz, wzi, zs, raw, a, send, recv, back, home, b, part, partial, total, final,
    load_sem, z_sem, z_out, y_sem, y_out, a_sem, a_out, h_sem, h_out, r_sem, r_out, f_sem, f_out, keep_sem,
):
    gz = lax.axis_index("gz")
    ta = lax.axis_index("ta")
    yl, q = gz // 8, gz % 8
    z, core = q // 2, q % 2
    yh, xc = ta // 4, ta % 4
    ym = yl * 2 + yh
    me = xc * 8 + q

    def plane(peer):
        return (yl * 8 + peer % 8, yh * 4 + peer // 8)

    def ring(member):
        return ((member // 2) * 8 + q, (member % 2) * 4 + xc)

    loads = [
        pltpu.make_async_copy(alpha_hbm, alpha, load_sem.at[0]),
        pltpu.make_async_copy(beta_hbm.at[yl], beta, load_sem.at[1]),
        pltpu.make_async_copy(wy_hbm.at[yh], wy, load_sem.at[2]),
        pltpu.make_async_copy(wx_hbm, wx, load_sem.at[3]),
        pltpu.make_async_copy(green, g, load_sem.at[4]),
        pltpu.make_async_copy(wxi_hbm, wxi, load_sem.at[5]),
        pltpu.make_async_copy(wyi_hbm.at[yh], wyi, load_sem.at[6]),
    ]
    for load in loads:
        load.start()

    barrier = pltpu.get_barrier_semaphore()

    def greet(step, carry):
        pl.semaphore_signal(barrier, inc=1, device_id=plane((me + step) % 32), device_id_type=MESH)
        return carry

    lax.fori_loop(1, 32, greet, 0)
    for step in range(1, 4):
        pl.semaphore_signal(barrier, inc=1, device_id=ring((ym + step) % 4), device_id_type=MESH)
    rows = charge.reshape(64 * 16, 128)
    for x in range(16):
        zs[x] = rows[pl.ds(x, 64, stride=16), :]
    pl.semaphore_wait(barrier, 34)

    for i in range(2):
        keep = pltpu.make_async_copy(
            zs.at[2 * q + i], raw.at[ym, i, z, pl.ds(core * 64, 64)], z_sem.at[i]
        )
        keep.start()

        def spread(step, carry):
            peer = (q + step) % 8
            pltpu.make_async_remote_copy(
                zs.at[2 * peer + i], raw.at[ym, i, z, pl.ds(core * 64, 64)], z_out, z_sem.at[i],
                device_id=(yl * 8 + peer, ta), device_id_type=MESH,
            ).start()
            return carry

        lax.fori_loop(1, 8, spread, 0)

    loads[0].wait()
    loads[1].wait()

    def build(slot, carry):
        turn = beta[slot]
        cos_b, sin_b = turn[0:1], turn[1:2]
        cos_a, sin_a = alpha[0], alpha[1]
        cosine = cos_a * cos_b - sin_a * sin_b
        sine = sin_a * cos_b + cos_a * sin_b
        blocks = []
        for k in range(2):
            c_k, s_k = cosine[k * 64 : k * 64 + 64], sine[k * 64 : k * 64 + 64]
            blocks += [jnp.concatenate([c_k, s_k], 1), jnp.concatenate([-s_k, c_k], 1)]
        table = jnp.concatenate(blocks, 0)
        high, low = split(table)
        wz[slot, 0] = high
        wz[slot, 1] = low
        odd = (slot % 2).astype(F32)
        wide = jnp.concatenate(
            [piece for block in blocks for piece in (block * (1.0 - odd), block * odd)], 0
        )
        high, low = split(wide.T)
        half = pl.multiple_of((slot % 2) * 256, 256)
        wzi[slot // 2, 0, pl.ds(half, 256), :] = high
        wzi[slot // 2, 1, pl.ds(half, 256), :] = low
        return carry

    lax.fori_loop(0, 8, build, 0)

    def ring_copy(i, step):
        return pltpu.make_async_remote_copy(
            raw.at[ym, i], raw.at[ym, i], y_out.at[i], y_sem.at[i, step - 1],
            device_id=ring((ym + step) % 4), device_id_type=MESH,
        )

    for i in range(2):
        pltpu.make_async_copy(raw.at[ym, i], raw.at[ym, i], z_sem.at[i]).wait()
        for step in (2, 1, 3):
            ring_copy(i, step).start()

    first = yl == 0
    sigma = jnp.where(first, 1.0, -1.0).astype(F32)

    def pick(zero, one):
        return jnp.where(first, np.float32(zero), np.float32(one))

    cos_t = [[pick(np.cos(np.pi * (e) * n / 8), np.cos(np.pi * (2 + e) * n / 8)) for n in range(4)] for e in range(2)]
    sin_t = [[pick(np.sin(np.pi * (e) * n / 8), np.sin(np.pi * (2 + e) * n / 8)) for n in range(4)] for e in range(2)]
    slots = (0, 2, 1, 3)

    def over_slabs(i):
        for row in range(2):

            def step(n, carry):
                at = pl.multiple_of(n * 16, 16)
                near = [raw[row, i, k, pl.ds(at, 16), :] for k in range(4)]
                far = [raw[2 + row, i, k, pl.ds(at, 16), :] for k in range(4)]
                for e in range(2):
                    re, im = [], []
                    for k in range(4):
                        ct, st = cos_t[e][k], sin_t[e][k]
                        if e == 0:
                            u = near[k] + sigma * far[k]
                            re.append(u * ct if k else u)
                            im.append(-(u * st) if k else jnp.zeros_like(u))
                        else:
                            w = sigma * far[k]
                            re.append(near[k] * ct - w * st if k else near[k])
                            im.append(-(near[k] * st + w * ct) if k else -w)
                    ar, ai = re[0] + re[2], im[0] + im[2]
                    br, bi = re[0] - re[2], im[0] - im[2]
                    cr, ci = re[1] + re[3], im[1] + im[3]
                    dr, di = re[1] - re[3], im[1] - im[3]
                    sums = [(ar + cr, ai + ci), (br + di, bi - dr), (ar - cr, ai - ci), (br - di, bi + dr)]
                    for j in range(4):
                        for c in range(2):
                            high, low = split(sums[j][c])
                            spot = pl.ds(pl.multiple_of(c * 128 + at, 16), 16)
                            a[slots[j], e, 0, spot, row * 128 : row * 128 + 128] = high
                            a[slots[j], e, 1, spot, row * 128 : row * 128 + 128] = low
                return carry

            lax.fori_loop(0, 8, step, 0)

    send_rows = send.reshape(32 * 256, 128)
    home_rows = home.reshape(32 * 256, 128)

    def forward_zy(i):
        def step(zt, carry):
            outs = []
            for e in range(2):
                weight = weight3(wz[zt * 2 + e, 0], wz[zt * 2 + e, 1])
                high, low = a[zt, e, 0], a[zt, e, 1]
                outs.append(dot_nn(weight, jnp.concatenate([high, low, high], 0)))
            for row in range(2):
                lanes = slice(row * 128, row * 128 + 128)
                field = jnp.concatenate(
                    [
                        jnp.concatenate([outs[e][k * 128 : k * 128 + 64, lanes], outs[e][k * 128 + 64 : k * 128 + 128, lanes]], 1)
                        for k in range(2)
                        for e in range(2)
                    ],
                    0,
                )
                plane_out = dot_nt(weight3(wy[0], wy[1]), data3(field, 1))
                for c in range(2):
                    for xt in range(4):
                        for k in range(2):
                            start = (xt * 8 + zt * 2 + k) * 256 + c * 4 + row * 2 + i
                            send_rows[pl.ds(start, 32, stride=8), :] = plane_out[
                                c * 128 + xt * 32 : c * 128 + xt * 32 + 32, k * 128 : k * 128 + 128
                            ]
            return carry

        lax.fori_loop(0, 4, step, 0)

    loads[2].wait()
    for i in range(2):
        for step in range(1, 4):
            ring_copy(i, step).wait_recv()
        over_slabs(i)
        forward_zy(i)

    my_rows = pl.ds(pl.multiple_of(me * 8, 8), 8)
    for chunk in range(CHUNKS):
        span = pl.ds(chunk * KY_STEP, KY_STEP)
        pltpu.make_async_copy(send.at[me, span], recv.at[span, my_rows], a_sem.at[chunk]).start()

        def exchange(step, carry):
            peer = (me + step) % 32
            pltpu.make_async_remote_copy(
                send.at[peer, span], recv.at[span, my_rows], a_out, a_sem.at[chunk],
                device_id=plane(peer), device_id_type=MESH,
            ).start()
            return carry

        lax.fori_loop(1, 32, exchange, 0)

    loads[3].wait()
    loads[4].wait()
    loads[5].wait()
    green_rows = g.reshape(256 * 32, 128)
    for chunk in range(CHUNKS):
        span = pl.ds(chunk * KY_STEP, KY_STEP)
        pltpu.make_async_copy(recv.at[span], recv.at[span], a_sem.at[chunk]).wait()

        def solve(n, carry):
            ky = chunk * KY_STEP + 2 * n
            field = jnp.concatenate([recv[ky], recv[ky + 1]], 1)
            full = dot_nn(weight3(wx[0], wx[1]), data3(field, 0))
            factor = jnp.concatenate(
                [green_rows[pl.ds(ky, 256, stride=32), :], green_rows[pl.ds(ky + 1, 256, stride=32), :]], 1
            )
            product = jnp.concatenate([full[:256] * factor, full[256:] * factor], 0)
            result = dot_nn(weight3(wxi[0], wxi[1]), data3(product, 0))
            back[ky] = result[:, :128]
            back[ky + 1] = result[:, 128:]
            return carry

        lax.fori_loop(0, KY_STEP // 2, solve, 0)
        pltpu.make_async_copy(back.at[span, my_rows], home.at[me, span], h_sem).start()

        def give_back(step, carry):
            peer = (me + step) % 32
            pltpu.make_async_remote_copy(
                back.at[span, pl.ds(pl.multiple_of(peer * 8, 8), 8)], home.at[me, span], h_out, h_sem,
                device_id=plane(peer), device_id_type=MESH,
            ).start()
            return carry

        lax.fori_loop(1, 32, give_back, 0)

    loads[6].wait()
    pltpu.make_async_copy(home, home, h_sem).wait()

    def inverse_yz(row):
        def step(zt, carry):
            pieces = []
            for i in range(2):
                columns = []
                for k in range(2):
                    blocks = []
                    for c in range(2):
                        for xt in range(4):
                            start = (xt * 8 + zt * 2 + k) * 256 + c * 4 + row * 2 + i
                            blocks.append(home_rows[pl.ds(start, 32, stride=8), :])
                    columns.append(jnp.concatenate(blocks, 0))
                along = dot_nn(weight3(wyi[0], wyi[1]), data3(jnp.concatenate(columns, 1), 0))
                pieces.append(
                    jnp.concatenate([along[c * 128 : c * 128 + 128, k * 128 : k * 128 + 128] for k in range(2) for c in range(2)], 1)
                )
            b[zt] = dot_nt(weight3(wzi[zt, 0], wzi[zt, 1]), data3(jnp.concatenate(pieces, 0), 1))
            return carry

        lax.fori_loop(0, 4, step, 0)

    def back_to_slabs(row):
        for i in range(2):
            lanes = slice(i * 128, i * 128 + 128)

            def step(n, carry):
                at = n * 8
                turned = []
                for e in range(2):
                    value = [
                        [b[slots[j], pl.ds(pl.multiple_of(e * 256 + c * 128 + at, 8), 8), lanes] for c in range(2)]
                        for j in range(4)
                    ]
                    (ar, ai), (br, bi), (cr, ci), (dr, di) = [
                        (value[l][0] + s * value[m][0], value[l][1] + s * value[m][1])
                        for l, m, s in ((0, 2, 1.0), (0, 2, -1.0), (1, 3, 1.0), (1, 3, -1.0))
                    ]
                    sums = [(ar + cr, ai + ci), (br - di, bi + dr), (ar - cr, ai - ci), (br + di, bi - dr)]
                    turned.append(
                        [
                            (re * cos_t[e][k] - im * sin_t[e][k], re * sin_t[e][k] + im * cos_t[e][k])
                            for k, (re, im) in enumerate(sums)
                        ]
                    )
                for k in range(4):
                    part[0, row, k, i, pl.ds(pl.multiple_of(at, 8), 8), :] = turned[0][k][0] + turned[1][k][0]
                    part[1, row, k, i, pl.ds(pl.multiple_of(at, 8), 8), :] = sigma * (turned[0][k][0] - turned[1][k][1])
                return carry

            lax.fori_loop(0, 16, step, 0)

    def sum_copy(member):
        return pltpu.make_async_remote_copy(
            part.at[member // 2, member % 2], partial.at[(ym - member) % 4 - 1], r_out, r_sem.at[(ym - member) % 4 - 1],
            device_id=ring(member), device_id_type=MESH,
        )

    other = 1 - yh
    inverse_yz(other)
    back_to_slabs(other)
    sum_copy(other).start()
    sum_copy(2 + other).start()
    inverse_yz(yh)
    back_to_slabs(yh)
    sum_copy((1 - yl) * 2 + yh).start()
    for step in range(3):
        pltpu.make_async_copy(partial.at[step], partial.at[step], r_sem.at[step]).wait()

    def add(n, carry):
        k, i = n // 2, n % 2
        total[k, i] = (part[yl, yh, k, i] + partial[0, k, i]) + (partial[1, k, i] + partial[2, k, i])
        return carry

    lax.fori_loop(0, 8, add, 0)
    pltpu.make_async_copy(total.at[z, :, pl.ds(core * 64, 64)], final.at[q], f_sem).start()

    def return_slab(step, carry):
        peer = (q + step) % 8
        pltpu.make_async_remote_copy(
            total.at[peer // 2, :, pl.ds((peer % 2) * 64, 64)], final.at[q], f_out, f_sem,
            device_id=(yl * 8 + peer, ta), device_id_type=MESH,
        ).start()
        return carry

    lax.fori_loop(1, 8, return_slab, 0)
    pltpu.make_async_copy(final, final, f_sem).wait()
    out_rows = out.reshape(64 * 16, 128)
    for x in range(16):
        out_rows[pl.ds(x, 64, stride=16), :] = final[x // 2, x % 2]

    def drain(ref, sem):
        pltpu.make_async_copy(ref, ref, sem).wait()

    drain(zs.at[pl.ds(0, 14)], z_out)
    for i in range(2):
        drain(raw.at[pl.ds(0, 3), i], y_out.at[i])
    drain(send.at[pl.ds(0, 31)], a_out)
    drain(send.at[pl.ds(0, 31)], h_out)
    drain(partial, r_out)
    drain(final.at[pl.ds(0, 7)], f_out)


def on_device(consts, charge, green_hat):
    any_spec = pl.BlockSpec(memory_space=pl.ANY)
    vmem_spec = pl.BlockSpec(memory_space=pltpu.VMEM)
    dma = pltpu.SemaphoreType.DMA
    return pl.pallas_call(
        kernel,
        out_shape=jax.ShapeDtypeStruct((64, 16, 128), F32),
        in_specs=[vmem_spec] + [any_spec] * 7,
        out_specs=vmem_spec,
        scratch_shapes=[
            pltpu.VMEM((256, 32, 128), F32),
            pltpu.VMEM((2, 512, 256), BF16),
            pltpu.VMEM((2, 256, 512), BF16),
            pltpu.VMEM((2, 256, 256), BF16),
            pltpu.VMEM((2, 256, 256), BF16),
            pltpu.VMEM((2, 128, 128), F32),
            pltpu.VMEM((8, 8, 128), F32),
            pltpu.VMEM((8, 2, 256, 256), BF16),
            pltpu.VMEM((4, 2, 512, 512), BF16),
            pltpu.VMEM((16, 64, 128), F32),
            pltpu.VMEM((4, 2, 4, 128, 128), F32),
            pltpu.VMEM((4, 2, 2, 256, 256), BF16),
            pltpu.VMEM((32, 32, 8, 128), F32),
            pltpu.VMEM((32, 256, 128), F32),
            pltpu.VMEM((32, 256, 128), F32),
            pltpu.VMEM((32, 32, 8, 128), F32),
            pltpu.VMEM((4, 512, 256), F32),
            pltpu.VMEM((2, 2, 4, 2, 128, 128), F32),
            pltpu.VMEM((3, 4, 2, 128, 128), F32),
            pltpu.VMEM((4, 2, 128, 128), F32),
            pltpu.VMEM((8, 2, 64, 128), F32),
            dma((7,)),
            dma((2,)),
            dma,
            dma((2, 3)),
            dma((2,)),
            dma((CHUNKS,)),
            dma,
            dma,
            dma,
            dma((3,)),
            dma,
            dma,
            dma,
            dma,
        ],
        compiler_params=pltpu.CompilerParams(
            collective_id=0, has_side_effects=True, vmem_limit_bytes=60 * 1024 * 1024
        ),
    )(charge, green_hat, *consts)


def solution(mesh):
    consts = tables()
    return jax.shard_map(
        functools.partial(on_device, consts),
        mesh=mesh,
        in_specs=(P("gz", "ta", None), P(None, "ta", "gz")),
        out_specs=P("gz", "ta", None),
        check_vma=False,
    )
```

```python
import functools

import jax
import jax.numpy as jnp
import ml_dtypes
import numpy as np
from jax import lax
from jax.experimental import pallas as pl
from jax.experimental.pallas import tpu as pltpu
from jax.sharding import PartitionSpec as P

MESH = pl.DeviceIdType.MESH
F32 = jnp.float32
BF16 = jnp.bfloat16
CHUNKS = 4
PAIR_STEP = 16 // CHUNKS


def halves(table):
    high = table.astype(ml_dtypes.bfloat16)
    low = (table - high.astype(np.float64)).astype(ml_dtypes.bfloat16)
    return np.stack([high, low])


def tables():
    peer = np.arange(32)
    pair = np.arange(2)
    x_of = (pair * 64)[None, None] + ((peer // 8) * 16 + (peer % 8) * 2)[None, :, None] + pair[:, None, None]
    kx = np.arange(256)
    angle = 2 * np.pi / 256 * (kx[:, None, None, None] * x_of[None] % 256)
    cosine, sine = np.cos(angle), np.sin(angle)
    wx = np.stack([np.stack([cosine, sine], 3), np.stack([-sine, cosine], 3)]).reshape(512, 256)
    y = np.arange(128)
    wy = []
    for y_half in range(2):
        ky = 128 * y_half + np.arange(128).reshape(4, 16, 2).transpose(0, 2, 1).reshape(128)
        angle = 2 * np.pi / 256 * (ky[:, None] * y[None] % 256)
        cosine, sine = np.cos(angle), np.sin(angle)
        wy.append(np.block([[cosine, sine], [-sine, cosine]]))
    wy = np.stack(wy)
    v = np.arange(128)
    low_bits = np.concatenate([2 * np.arange(64), 2 * np.arange(64) + 1])
    angle = 2 * np.pi / 128 * (low_bits[:, None] * v[None] % 128)
    alpha = np.stack([np.cos(angle), np.sin(angle)]).astype(np.float32)
    reverse = np.array([0, 2, 1, 3])
    s = 4 * reverse[None, :, None] + 2 * np.arange(2)[:, None, None] + np.arange(2)[None, None]
    angle = 2 * np.pi / 2048 * (s.reshape(2, 8)[..., None] * v % 2048)
    beta = np.stack([np.cos(angle), np.sin(angle)], 2).astype(np.float32)
    beta = np.pad(beta, ((0, 0), (0, 0), (0, 6), (0, 0)))
    return (
        halves(wx),
        halves(wx.T * 2.0**-27),
        np.stack([halves(w) for w in wy]),
        np.stack([halves(w.T) for w in wy]),
        alpha,
        beta,
    )


def split(value):
    high = value.astype(BF16)
    return high, (value - high.astype(F32)).astype(BF16)


def weight3(high, low):
    return jnp.concatenate([high, high, low], axis=1)


def data3(value, axis):
    high, low = split(value)
    return jnp.concatenate([high, low, high], axis=axis)


def dot_nn(weight, data):
    return jnp.dot(weight, data, preferred_element_type=F32)


def dot_nt(weight, data):
    return lax.dot_general(weight, data, (((1,), (1,)), ((), ())), preferred_element_type=F32)


def kernel(
    charge, green, wx_hbm, wxi_hbm, wy_hbm, wyi_hbm, alpha_hbm, beta_hbm,
    out,
    g, wx, wxi, wy, wyi, alpha, beta, wz, wzi, zs, raw, a, send, recv, back, home, b, part, partial, total, final,
    load_sem, z_sem, z_out, y_sem, y_out, a_sem, a_out, h_sem, h_out, r_sem, r_out, f_sem, f_out,
):
    gz = lax.axis_index("gz")
    ta = lax.axis_index("ta")
    yl, q = gz // 8, gz % 8
    z, core = q // 2, q % 2
    yh, xc = ta // 4, ta % 4
    ym = yl * 2 + yh
    me = xc * 8 + q

    def plane(peer):
        return (yl * 8 + peer % 8, yh * 4 + peer // 8)

    def ring(member):
        return ((member // 2) * 8 + q, (member % 2) * 4 + xc)

    loads = [
        pltpu.make_async_copy(alpha_hbm, alpha, load_sem.at[0]),
        pltpu.make_async_copy(beta_hbm.at[yl], beta, load_sem.at[1]),
        pltpu.make_async_copy(wy_hbm.at[yh], wy, load_sem.at[2]),
        pltpu.make_async_copy(wx_hbm, wx, load_sem.at[3]),
        pltpu.make_async_copy(green, g, load_sem.at[4]),
        pltpu.make_async_copy(wxi_hbm, wxi, load_sem.at[5]),
        pltpu.make_async_copy(wyi_hbm.at[yh], wyi, load_sem.at[6]),
    ]
    for load in loads:
        load.start()

    barrier = pltpu.get_barrier_semaphore()

    def greet(step, carry):
        pl.semaphore_signal(barrier, inc=1, device_id=plane((me + step) % 32), device_id_type=MESH)
        return carry

    lax.fori_loop(1, 32, greet, 0)
    for step in range(1, 4):
        pl.semaphore_signal(barrier, inc=1, device_id=ring((ym + step) % 4), device_id_type=MESH)
    rows = charge.reshape(64 * 16, 128)
    for x in range(16):
        zs[x] = rows[pl.ds(x, 64, stride=16), :]
    pl.semaphore_wait(barrier, 34)

    for i in range(2):
        keep = pltpu.make_async_copy(
            zs.at[2 * q + i], raw.at[ym, i, z, pl.ds(core * 64, 64)], z_sem.at[i]
        )
        keep.start()

        def spread(step, carry):
            peer = (q + step) % 8
            pltpu.make_async_remote_copy(
                zs.at[2 * peer + i], raw.at[ym, i, z, pl.ds(core * 64, 64)], z_out, z_sem.at[i],
                device_id=(yl * 8 + peer, ta), device_id_type=MESH,
            ).start()
            return carry

        lax.fori_loop(1, 8, spread, 0)

    loads[0].wait()
    loads[1].wait()

    def build(slot, carry):
        turn = beta[slot]
        cos_b, sin_b = turn[0:1], turn[1:2]
        cos_a, sin_a = alpha[0], alpha[1]
        cosine = cos_a * cos_b - sin_a * sin_b
        sine = sin_a * cos_b + cos_a * sin_b
        blocks = []
        for k in range(2):
            c_k, s_k = cosine[k * 64 : k * 64 + 64], sine[k * 64 : k * 64 + 64]
            blocks += [jnp.concatenate([c_k, s_k], 1), jnp.concatenate([-s_k, c_k], 1)]
        table = jnp.concatenate(blocks, 0)
        high, low = split(table)
        wz[slot, 0] = high
        wz[slot, 1] = low
        odd = (slot % 2).astype(F32)
        wide = jnp.concatenate(
            [piece for block in blocks for piece in (block * (1.0 - odd), block * odd)], 0
        )
        high, low = split(wide.T)
        half = pl.multiple_of((slot % 2) * 256, 256)
        wzi[slot // 2, 0, pl.ds(half, 256), :] = high
        wzi[slot // 2, 1, pl.ds(half, 256), :] = low
        return carry

    lax.fori_loop(0, 8, build, 0)

    def ring_copy(i, step):
        return pltpu.make_async_remote_copy(
            raw.at[ym, i], raw.at[ym, i], y_out.at[i], y_sem.at[i, step - 1],
            device_id=ring((ym + step) % 4), device_id_type=MESH,
        )

    for i in range(2):
        pltpu.make_async_copy(raw.at[ym, i], raw.at[ym, i], z_sem.at[i]).wait()
        for step in (2, 1, 3):
            ring_copy(i, step).start()

    first = yl == 0
    sigma = jnp.where(first, 1.0, -1.0).astype(F32)

    def pick(zero, one):
        return jnp.where(first, np.float32(zero), np.float32(one))

    cos_t = [[pick(np.cos(np.pi * (e) * n / 8), np.cos(np.pi * (2 + e) * n / 8)) for n in range(4)] for e in range(2)]
    sin_t = [[pick(np.sin(np.pi * (e) * n / 8), np.sin(np.pi * (2 + e) * n / 8)) for n in range(4)] for e in range(2)]
    slots = (0, 2, 1, 3)

    def over_slabs(i):
        for row in range(2):

            def step(n, carry):
                at = pl.multiple_of(n * 16, 16)
                near = [raw[row, i, k, pl.ds(at, 16), :] for k in range(4)]
                far = [raw[2 + row, i, k, pl.ds(at, 16), :] for k in range(4)]
                for e in range(2):
                    re, im = [], []
                    for k in range(4):
                        ct, st = cos_t[e][k], sin_t[e][k]
                        if e == 0:
                            u = near[k] + sigma * far[k]
                            re.append(u * ct if k else u)
                            im.append(-(u * st) if k else jnp.zeros_like(u))
                        else:
                            w = sigma * far[k]
                            re.append(near[k] * ct - w * st if k else near[k])
                            im.append(-(near[k] * st + w * ct) if k else -w)
                    ar, ai = re[0] + re[2], im[0] + im[2]
                    br, bi = re[0] - re[2], im[0] - im[2]
                    cr, ci = re[1] + re[3], im[1] + im[3]
                    dr, di = re[1] - re[3], im[1] - im[3]
                    sums = [(ar + cr, ai + ci), (br + di, bi - dr), (ar - cr, ai - ci), (br - di, bi + dr)]
                    for j in range(4):
                        for c in range(2):
                            high, low = split(sums[j][c])
                            spot = pl.ds(pl.multiple_of(c * 128 + at, 16), 16)
                            a[slots[j], e, 0, spot, row * 128 : row * 128 + 128] = high
                            a[slots[j], e, 1, spot, row * 128 : row * 128 + 128] = low
                return carry

            lax.fori_loop(0, 8, step, 0)

    send_rows = send.reshape(2 * 32 * 128, 128)
    home_rows = home.reshape(2 * 32 * 128, 128)
    my_first = pl.ds(pl.multiple_of(me * 8, 8), 8)
    my_second = pl.ds(pl.multiple_of(256 + me * 8, 8), 8)

    def partner(step):
        turn = step // 2
        return ((xc + turn) % 4) * 8 + ((z + turn // 4 + turn) % 4) * 2 + (core + step) % 2


    def first_copy(peer):
        return pltpu.make_async_remote_copy(
            send.at[0, peer], recv.at[:, my_first], a_out.at[0], a_sem.at[CHUNKS], device_id=plane(peer), device_id_type=MESH
        )

    def send_first(zt, mine):
        def step(n, carry):
            peer = ((xc + n // 2) % 4) * 8 + zt * 2 + (core + n) % 2
            keep = jnp.logical_and(mine, n == 0)

            @pl.when(keep)
            def _():
                pltpu.make_async_copy(send.at[0, me], recv.at[:, my_first], a_sem.at[CHUNKS]).start()

            @pl.when(jnp.logical_not(keep))
            def _():
                first_copy(peer).start()

            return carry

        lax.fori_loop(0, 8, step, 0)

    def forward_zy(i):
        def step(n, carry):
            zt = (z + n) % 4
            outs = []
            for e in range(2):
                weight = weight3(wz[zt * 2 + e, 0], wz[zt * 2 + e, 1])
                high, low = a[zt, e, 0], a[zt, e, 1]
                outs.append(dot_nn(weight, jnp.concatenate([high, low, high], 0)))
            for row in range(2):
                lanes = slice(row * 128, row * 128 + 128)
                field = jnp.concatenate(
                    [
                        jnp.concatenate([outs[e][k * 128 : k * 128 + 64, lanes], outs[e][k * 128 + 64 : k * 128 + 128, lanes]], 1)
                        for k in range(2)
                        for e in range(2)
                    ],
                    0,
                )
                plane_out = dot_nt(weight3(wy[0], wy[1]), data3(field, 1))
                for c in range(2):
                    for xt in range(4):
                        for odd in range(2):
                            at = c * 128 + xt * 32 + odd * 16
                            for k in range(2):
                                start = (i * 32 + xt * 8 + zt * 2 + k) * 128 + c * 4 + row * 2 + odd
                                send_rows[pl.ds(start, 16, stride=8), :] = plane_out[
                                    at : at + 16, k * 128 : k * 128 + 128
                                ]
            if i == 0:

                @pl.when(n > 0)
                def _():
                    send_first((z + n - 1) % 4, n == 1)

            return carry

        lax.fori_loop(0, 4, step, 0)
        if i == 0:
            send_first((z + 3) % 4, False)

    loads[2].wait()
    for i in range(2):
        for step in range(1, 4):
            ring_copy(i, step).wait_recv()
        over_slabs(i)
        forward_zy(i)

    for chunk in range(CHUNKS):
        span = pl.ds(chunk * PAIR_STEP, PAIR_STEP)
        pltpu.make_async_copy(send.at[1, me, span], recv.at[span, my_second], a_sem.at[chunk]).start()

        def exchange(step, carry):
            peer = partner(step)
            pltpu.make_async_remote_copy(
                send.at[1, peer, span], recv.at[span, my_second], a_out.at[1], a_sem.at[chunk],
                device_id=plane(peer), device_id_type=MESH,
            ).start()
            return carry

        lax.fori_loop(1, 32, exchange, 0)

    loads[3].wait()
    loads[4].wait()
    loads[5].wait()
    green_rows = g.reshape(256 * 32, 128)
    recv_rows = recv.reshape(16 * 512, 128)
    back_rows = back.reshape(16 * 512, 128)

    def give_back(i, span):
        mine = pl.ds(pl.multiple_of(i * 256 + me * 8, 8), 8)
        pltpu.make_async_copy(back.at[span, mine], home.at[i, me, span], h_sem.at[i]).start()

        def step(n, carry):
            peer = partner(n)
            pltpu.make_async_remote_copy(
                back.at[span, pl.ds(pl.multiple_of(i * 256 + peer * 8, 8), 8)], home.at[i, me, span],
                h_out.at[i], h_sem.at[i], device_id=plane(peer), device_id_type=MESH,
            ).start()
            return carry

        lax.fori_loop(1, 32, step, 0)

    whole = recv.at[:, pl.ds(0, 256)]
    pltpu.make_async_copy(whole, whole, a_sem.at[CHUNKS]).wait()
    for chunk in range(CHUNKS):
        span = pl.ds(chunk * PAIR_STEP, PAIR_STEP)
        arrived = recv.at[span, pl.ds(256, 256)]
        pltpu.make_async_copy(arrived, arrived, a_sem.at[chunk]).wait()

        def solve(n, carry):
            pair = chunk * PAIR_STEP + n
            field = jnp.concatenate([recv_rows[pl.ds(pair * 512 + odd, 256, stride=2), :] for odd in range(2)], 1)
            full = dot_nn(weight3(wx[0], wx[1]), data3(field, 0))
            factor = jnp.concatenate([green_rows[pl.ds(2 * pair + odd, 256, stride=32), :] for odd in range(2)], 1)
            product = jnp.concatenate([full[:256] * factor, full[256:] * factor], 0)
            result = dot_nn(weight3(wxi[0], wxi[1]), data3(product, 0))
            for odd in range(2):
                back_rows[pl.ds(pair * 512 + odd, 256, stride=2), :] = result[:, odd * 128 : odd * 128 + 128]
            return carry

        lax.fori_loop(0, PAIR_STEP, solve, 0)
        give_back(0, span)
    give_back(1, pl.ds(0, 16))

    loads[6].wait()

    def inverse_yz(i):
        def step(zt, carry):
            pieces = []
            for row in range(2):
                columns = []
                for k in range(2):
                    blocks = []
                    for c in range(2):
                        for xt in range(4):
                            for odd in range(2):
                                start = (i * 32 + xt * 8 + zt * 2 + k) * 128 + c * 4 + row * 2 + odd
                                blocks.append(home_rows[pl.ds(start, 16, stride=8), :])
                    columns.append(jnp.concatenate(blocks, 0))
                along = dot_nn(weight3(wyi[0], wyi[1]), data3(jnp.concatenate(columns, 1), 0))
                pieces.append(
                    jnp.concatenate([along[c * 128 : c * 128 + 128, k * 128 : k * 128 + 128] for k in range(2) for c in range(2)], 1)
                )
            b[zt] = dot_nt(weight3(wzi[zt, 0], wzi[zt, 1]), data3(jnp.concatenate(pieces, 0), 1))
            return carry

        lax.fori_loop(0, 4, step, 0)

    def back_to_slabs(i, row):
        for lanes in (pl.ds(pl.multiple_of(row * 128, 128), 128),):

            def step(n, carry):
                at = n * 8
                turned = []
                for e in range(2):
                    value = [
                        [b[slots[j], pl.ds(pl.multiple_of(e * 256 + c * 128 + at, 8), 8), lanes] for c in range(2)]
                        for j in range(4)
                    ]
                    (ar, ai), (br, bi), (cr, ci), (dr, di) = [
                        (value[l][0] + s * value[m][0], value[l][1] + s * value[m][1])
                        for l, m, s in ((0, 2, 1.0), (0, 2, -1.0), (1, 3, 1.0), (1, 3, -1.0))
                    ]
                    sums = [(ar + cr, ai + ci), (br - di, bi + dr), (ar - cr, ai - ci), (br + di, bi - dr)]
                    turned.append(
                        [
                            (re * cos_t[e][k] - im * sin_t[e][k], re * sin_t[e][k] + im * cos_t[e][k])
                            for k, (re, im) in enumerate(sums)
                        ]
                    )
                for k in range(4):
                    part[0, row, i, k, pl.ds(pl.multiple_of(at, 8), 8), :] = turned[0][k][0] + turned[1][k][0]
                    part[1, row, i, k, pl.ds(pl.multiple_of(at, 8), 8), :] = sigma * (turned[0][k][0] - turned[1][k][1])
                return carry

            lax.fori_loop(0, 16, step, 0)

    def sum_copy(i, member):
        slot = (ym - member) % 4 - 1
        return pltpu.make_async_remote_copy(
            part.at[member // 2, member % 2, i], partial.at[slot, i], r_out.at[i], r_sem.at[i, slot],
            device_id=ring(member), device_id_type=MESH,
        )

    other = 1 - yh

    def home_half(i):
        pltpu.make_async_copy(home.at[i], home.at[i], h_sem.at[i]).wait()
        inverse_yz(i)
        back_to_slabs(i, other)
        sum_copy(i, other).start()
        sum_copy(i, 2 + other).start()
        back_to_slabs(i, yh)
        sum_copy(i, (1 - yl) * 2 + yh).start()

    def finish(i):
        for step in range(3):
            pltpu.make_async_copy(partial.at[step, i], partial.at[step, i], r_sem.at[i, step]).wait()

        def add(k, carry):
            total[k, i] = (part[yl, yh, i, k] + partial[0, i, k]) + (partial[1, i, k] + partial[2, i, k])
            return carry

        lax.fori_loop(0, 4, add, 0)
        pltpu.make_async_copy(total.at[z, i, pl.ds(core * 64, 64)], final.at[q, i], f_sem.at[i]).start()

        def return_slab(step, carry):
            peer = (q + step) % 8
            pltpu.make_async_remote_copy(
                total.at[peer // 2, i, pl.ds((peer % 2) * 64, 64)], final.at[q, i], f_out.at[i], f_sem.at[i],
                device_id=(yl * 8 + peer, ta), device_id_type=MESH,
            ).start()
            return carry

        lax.fori_loop(1, 8, return_slab, 0)

    home_half(0)
    finish(0)
    home_half(1)
    finish(1)
    out_rows = out.reshape(64 * 16, 128)
    for i in range(2):
        pltpu.make_async_copy(final.at[:, i], final.at[:, i], f_sem.at[i]).wait()
        for n in range(8):
            out_rows[pl.ds(2 * n + i, 64, stride=16), :] = final[n, i]

    def drain(ref, sem):
        pltpu.make_async_copy(ref, ref, sem).wait()

    drain(zs.at[pl.ds(0, 14)], z_out)
    for i in range(2):
        drain(raw.at[pl.ds(0, 3), i], y_out.at[i])
    for i in range(2):
        drain(send.at[i, pl.ds(0, 31)], a_out.at[i])
        drain(send.at[i, pl.ds(0, 31)], h_out.at[i])
        drain(partial.at[:, i], r_out.at[i])
        drain(final.at[pl.ds(0, 7), i], f_out.at[i])


def on_device(consts, charge, green_hat):
    any_spec = pl.BlockSpec(memory_space=pl.ANY)
    vmem_spec = pl.BlockSpec(memory_space=pltpu.VMEM)
    dma = pltpu.SemaphoreType.DMA
    return pl.pallas_call(
        kernel,
        out_shape=jax.ShapeDtypeStruct((64, 16, 128), F32),
        in_specs=[vmem_spec] + [any_spec] * 7,
        out_specs=vmem_spec,
        scratch_shapes=[
            pltpu.VMEM((256, 32, 128), F32),
            pltpu.VMEM((2, 512, 256), BF16),
            pltpu.VMEM((2, 256, 512), BF16),
            pltpu.VMEM((2, 256, 256), BF16),
            pltpu.VMEM((2, 256, 256), BF16),
            pltpu.VMEM((2, 128, 128), F32),
            pltpu.VMEM((8, 8, 128), F32),
            pltpu.VMEM((8, 2, 256, 256), BF16),
            pltpu.VMEM((4, 2, 512, 512), BF16),
            pltpu.VMEM((16, 64, 128), F32),
            pltpu.VMEM((4, 2, 4, 128, 128), F32),
            pltpu.VMEM((4, 2, 2, 256, 256), BF16),
            pltpu.VMEM((2, 32, 16, 8, 128), F32),
            pltpu.VMEM((16, 512, 128), F32),
            pltpu.VMEM((16, 512, 128), F32),
            pltpu.VMEM((2, 32, 16, 8, 128), F32),
            pltpu.VMEM((4, 512, 256), F32),
            pltpu.VMEM((2, 2, 2, 4, 128, 128), F32),
            pltpu.VMEM((3, 2, 4, 128, 128), F32),
            pltpu.VMEM((4, 2, 128, 128), F32),
            pltpu.VMEM((8, 2, 64, 128), F32),
            dma((7,)),
            dma((2,)),
            dma,
            dma((2, 3)),
            dma((2,)),
            dma((CHUNKS + 1,)),
            dma((2,)),
            dma((2,)),
            dma((2,)),
            dma((2, 3)),
            dma((2,)),
            dma((2,)),
            dma((2,)),
        ],
        compiler_params=pltpu.CompilerParams(
            collective_id=0, has_side_effects=True, vmem_limit_bytes=60 * 1024 * 1024
        ),
    )(charge, green_hat, *consts)


def solution(mesh):
    consts = tables()
    return jax.shard_map(
        functools.partial(on_device, consts),
        mesh=mesh,
        in_specs=(P("gz", "ta", None), P(None, "ta", "gz")),
        out_specs=P("gz", "ta", None),
        check_vma=False,
    )
```

```python
import functools

import jax
import jax.numpy as jnp
import ml_dtypes
import numpy as np
from jax import lax
from jax.experimental import pallas as pl
from jax.experimental.pallas import tpu as pltpu
from jax.sharding import PartitionSpec as P

MESH = pl.DeviceIdType.MESH
F32 = jnp.float32
BF16 = jnp.bfloat16
CHUNKS = 4
QUADS = 8 // CHUNKS


def halves(table):
    high = table.astype(ml_dtypes.bfloat16)
    low = (table - high.astype(np.float64)).astype(ml_dtypes.bfloat16)
    return np.stack([high, low])


def tables():
    peer = np.arange(32)
    row = np.arange(4)
    x_of = ((peer // 8) * 16 + (peer % 8) * 2)[None, :] + ((row // 2) * 64 + row % 2)[:, None]
    kx = np.arange(256)
    angle = 2 * np.pi / 256 * (kx[:, None, None] * x_of[None] % 256)
    cosine, sine = np.cos(angle), np.sin(angle)
    wx = np.stack([np.stack([cosine, sine], 3), np.stack([-sine, cosine], 3)]).reshape(512, 256)
    y = np.arange(128)
    wy = []
    for y_half in range(2):
        ky = 128 * y_half + np.arange(128).reshape(4, 8, 4).transpose(0, 2, 1).reshape(128)
        angle = 2 * np.pi / 256 * (ky[:, None] * y[None] % 256)
        cosine, sine = np.cos(angle), np.sin(angle)
        wy.append(np.block([[cosine, sine], [-sine, cosine]]))
    wy = np.stack(wy)
    v = np.arange(128)
    low_bits = np.concatenate([2 * np.arange(64), 2 * np.arange(64) + 1])
    angle = 2 * np.pi / 128 * (low_bits[:, None] * v[None] % 128)
    alpha = np.stack([np.cos(angle), np.sin(angle)]).astype(np.float32)
    reverse = np.array([0, 2, 1, 3])
    s = 4 * reverse[None, :, None] + 2 * np.arange(2)[:, None, None] + np.arange(2)[None, None]
    angle = 2 * np.pi / 2048 * (s.reshape(2, 8)[..., None] * v % 2048)
    beta = np.stack([np.cos(angle), np.sin(angle)], 2).astype(np.float32)
    beta = np.pad(beta, ((0, 0), (0, 0), (0, 6), (0, 0)))
    return (
        halves(wx),
        halves(wx.T * 2.0**-27),
        np.stack([halves(w) for w in wy]),
        np.stack([halves(w.T) for w in wy]),
        alpha,
        beta,
    )


def split(value):
    high = value.astype(BF16)
    return high, (value - high.astype(F32)).astype(BF16)


def weight3(high, low):
    return jnp.concatenate([high, high, low], axis=1)


def data3(value, axis):
    high, low = split(value)
    return jnp.concatenate([high, low, high], axis=axis)


def dot_nn(weight, data):
    return jnp.dot(weight, data, preferred_element_type=F32)


def dot_nt(weight, data):
    return lax.dot_general(weight, data, (((1,), (1,)), ((), ())), preferred_element_type=F32)


def kernel(
    charge, green, wx_hbm, wxi_hbm, wy_hbm, wyi_hbm, alpha_hbm, beta_hbm,
    out,
    g, wx, wxi, wy, wyi, alpha, beta, wz, wzi, zs, raw, a, send, recv, back, home, b, part, partial, total, final,
    load_sem, z_sem, z_out, y_sem, y_out, a_sem, a_out, h_sem, h_out, r_sem, r_out, f_sem, f_out,
):
    gz = lax.axis_index("gz")
    ta = lax.axis_index("ta")
    yl, q = gz // 8, gz % 8
    z, core = q // 2, q % 2
    yh, xc = ta // 4, ta % 4
    ym = yl * 2 + yh
    me = xc * 8 + q

    def plane(peer):
        return (yl * 8 + peer % 8, yh * 4 + peer // 8)

    def ring(member):
        return ((member // 2) * 8 + q, (member % 2) * 4 + xc)

    loads = [
        pltpu.make_async_copy(alpha_hbm, alpha, load_sem.at[0]),
        pltpu.make_async_copy(beta_hbm.at[yl], beta, load_sem.at[1]),
        pltpu.make_async_copy(wy_hbm.at[yh], wy, load_sem.at[2]),
        pltpu.make_async_copy(wx_hbm, wx, load_sem.at[3]),
        pltpu.make_async_copy(green, g, load_sem.at[4]),
        pltpu.make_async_copy(wxi_hbm, wxi, load_sem.at[5]),
        pltpu.make_async_copy(wyi_hbm.at[yh], wyi, load_sem.at[6]),
    ]
    for load in loads:
        load.start()

    barrier = pltpu.get_barrier_semaphore()

    def greet(step, carry):
        pl.semaphore_signal(barrier, inc=1, device_id=plane((me + step) % 32), device_id_type=MESH)
        return carry

    lax.fori_loop(1, 32, greet, 0)
    for step in range(1, 4):
        pl.semaphore_signal(barrier, inc=1, device_id=ring((ym + step) % 4), device_id_type=MESH)
    rows = charge.reshape(64 * 16, 128)
    for x in range(16):
        zs[x] = rows[pl.ds(x, 64, stride=16), :]
    pl.semaphore_wait(barrier, 34)

    for i in range(2):
        keep = pltpu.make_async_copy(
            zs.at[2 * q + i], raw.at[ym, i, z, pl.ds(core * 64, 64)], z_sem.at[i]
        )
        keep.start()

        def spread(step, carry):
            peer = (q + step) % 8
            pltpu.make_async_remote_copy(
                zs.at[2 * peer + i], raw.at[ym, i, z, pl.ds(core * 64, 64)], z_out, z_sem.at[i],
                device_id=(yl * 8 + peer, ta), device_id_type=MESH,
            ).start()
            return carry

        lax.fori_loop(1, 8, spread, 0)

    loads[0].wait()
    loads[1].wait()

    def build(slot, carry):
        turn = beta[slot]
        cos_b, sin_b = turn[0:1], turn[1:2]
        cos_a, sin_a = alpha[0], alpha[1]
        cosine = cos_a * cos_b - sin_a * sin_b
        sine = sin_a * cos_b + cos_a * sin_b
        blocks = []
        for k in range(2):
            c_k, s_k = cosine[k * 64 : k * 64 + 64], sine[k * 64 : k * 64 + 64]
            blocks += [jnp.concatenate([c_k, s_k], 1), jnp.concatenate([-s_k, c_k], 1)]
        table = jnp.concatenate(blocks, 0)
        high, low = split(table)
        wz[slot, 0] = high
        wz[slot, 1] = low
        odd = (slot % 2).astype(F32)
        wide = jnp.concatenate(
            [piece for block in blocks for piece in (block * (1.0 - odd), block * odd)], 0
        )
        high, low = split(wide.T)
        half = pl.multiple_of((slot % 2) * 256, 256)
        wzi[slot // 2, 0, pl.ds(half, 256), :] = high
        wzi[slot // 2, 1, pl.ds(half, 256), :] = low
        return carry

    lax.fori_loop(0, 8, build, 0)

    def ring_copy(i, step):
        return pltpu.make_async_remote_copy(
            raw.at[ym, i], raw.at[ym, i], y_out.at[i], y_sem.at[i, step - 1],
            device_id=ring((ym + step) % 4), device_id_type=MESH,
        )

    for i in range(2):
        pltpu.make_async_copy(raw.at[ym, i], raw.at[ym, i], z_sem.at[i]).wait()
        ring_copy(i, 2).start()
    for i in range(2):
        for step in (1, 3):
            ring_copy(i, step).start()

    first = yl == 0
    sigma = jnp.where(first, 1.0, -1.0).astype(F32)

    def pick(zero, one):
        return jnp.where(first, np.float32(zero), np.float32(one))

    cos_t = [[pick(np.cos(np.pi * (e) * n / 8), np.cos(np.pi * (2 + e) * n / 8)) for n in range(4)] for e in range(2)]
    sin_t = [[pick(np.sin(np.pi * (e) * n / 8), np.sin(np.pi * (2 + e) * n / 8)) for n in range(4)] for e in range(2)]
    slots = (0, 2, 1, 3)

    def over_slabs(row, i):
        for _ in range(1):

            def step(n, carry):
                at = pl.multiple_of(n * 16, 16)
                near = [raw[row, i, k, pl.ds(at, 16), :] for k in range(4)]
                far = [raw[2 + row, i, k, pl.ds(at, 16), :] for k in range(4)]
                for e in range(2):
                    re, im = [], []
                    for k in range(4):
                        ct, st = cos_t[e][k], sin_t[e][k]
                        if e == 0:
                            u = near[k] + sigma * far[k]
                            re.append(u * ct if k else u)
                            im.append(-(u * st) if k else jnp.zeros_like(u))
                        else:
                            w = sigma * far[k]
                            re.append(near[k] * ct - w * st if k else near[k])
                            im.append(-(near[k] * st + w * ct) if k else -w)
                    ar, ai = re[0] + re[2], im[0] + im[2]
                    br, bi = re[0] - re[2], im[0] - im[2]
                    cr, ci = re[1] + re[3], im[1] + im[3]
                    dr, di = re[1] - re[3], im[1] - im[3]
                    sums = [(ar + cr, ai + ci), (br + di, bi - dr), (ar - cr, ai - ci), (br - di, bi + dr)]
                    for j in range(4):
                        for c in range(2):
                            high, low = split(sums[j][c])
                            spot = pl.ds(pl.multiple_of(c * 128 + at, 16), 16)
                            a[slots[j], e, 0, spot, :] = high
                            a[slots[j], e, 1, spot, :] = low
                return carry

            lax.fori_loop(0, 8, step, 0)

    send_rows = send.reshape(4 * 32 * 64, 128)
    home_rows = home.reshape(32 * 256, 128)
    mine = pl.ds(pl.multiple_of(me * 8, 8), 8)

    def partner(step):
        turn = step // 2
        return ((xc + turn) % 4) * 8 + ((z + turn // 4 + turn) % 4) * 2 + (core + step) % 2


    def plane_copy(line, peer, span, slot, sem):
        return pltpu.make_async_remote_copy(
            send.at[line, peer, span], recv.at[span, line, mine], a_out.at[slot], sem,
            device_id=plane(peer), device_id_type=MESH,
        )

    def plane_keep(line, span, sem):
        pltpu.make_async_copy(send.at[line, me, span], recv.at[span, line, mine], sem).start()

    def send_first(line, zt, here):
        def step(n, carry):
            peer = ((xc + n // 2) % 4) * 8 + zt * 2 + (core + n) % 2
            keep = jnp.logical_and(here, n == 0)

            @pl.when(keep)
            def _():
                plane_keep(line, pl.ds(0, 8), a_sem.at[0])

            @pl.when(jnp.logical_not(keep))
            def _():
                plane_copy(line, peer, pl.ds(0, 8), 0, a_sem.at[0]).start()

            return carry

        lax.fori_loop(0, 8, step, 0)

    def send_line(order, line, span, sem):
        plane_keep(line, span, sem)

        def step(n, carry):
            plane_copy(line, partner(n), span, order, sem).start()
            return carry

        lax.fori_loop(1, 32, step, 0)

    def far_first(n):
        return (z + jnp.where(n == 0, 2, jnp.where(n == 1, 1, jnp.where(n == 2, 3, 0)))) % 4

    def forward_zy(order, line):
        def step(n, carry):
            zt = far_first(n)
            outs = []
            for e in range(2):
                weight = weight3(wz[zt * 2 + e, 0], wz[zt * 2 + e, 1])
                high, low = a[zt, e, 0], a[zt, e, 1]
                outs.append(dot_nn(weight, jnp.concatenate([high, low, high], 0)))
            field = jnp.concatenate(
                [
                    jnp.concatenate([outs[e][k * 128 : k * 128 + 64], outs[e][k * 128 + 64 : k * 128 + 128]], 1)
                    for k in range(2)
                    for e in range(2)
                ],
                0,
            )
            plane_out = dot_nt(weight3(wy[0], wy[1]), data3(field, 1))
            for c in range(2):
                for xt in range(4):
                    for r in range(4):
                        at = c * 128 + xt * 32 + r * 8
                        for k in range(2):
                            start = (line * 32 + xt * 8 + zt * 2 + k) * 64 + c * 4 + r
                            send_rows[pl.ds(start, 8, stride=8), :] = plane_out[at : at + 8, k * 128 : k * 128 + 128]
            if order == 0:

                @pl.when(n > 0)
                def _():
                    send_first(line, far_first(n - 1), False)

            return carry

        lax.fori_loop(0, 4, step, 0)
        if order == 0:
            send_first(line, far_first(3), True)
        elif order < 3:
            send_line(order, line, pl.ds(0, 8), a_sem.at[order])

    loads[2].wait()
    other = 1 - yh
    lines = ((yh, 0), (yh, 1), (other, 0), (other, 1))
    for order, (row, i) in enumerate(lines):
        for step in ((2,) if order < 2 else (1, 3)):
            ring_copy(i, step).wait_recv()
        over_slabs(row, i)
        forward_zy(order, row * 2 + i)

    last = other * 2 + 1
    for chunk in range(CHUNKS):
        send_line(3, last, pl.ds(chunk * QUADS, QUADS), a_sem.at[3 + chunk])

    loads[3].wait()
    loads[4].wait()
    loads[5].wait()
    green_rows = g.reshape(256 * 32, 128)
    recv_rows = recv.reshape(8 * 1024, 128)
    back_rows = back.reshape(8 * 1024, 128)

    def give_back(slot, lines_of, span):
        pltpu.make_async_copy(back.at[span, lines_of, mine], home.at[me, span, lines_of], h_sem.at[slot]).start()

        def step(n, carry):
            peer = partner(n)
            pltpu.make_async_remote_copy(
                back.at[span, lines_of, pl.ds(pl.multiple_of(peer * 8, 8), 8)], home.at[me, span, lines_of],
                h_out.at[slot], h_sem.at[slot], device_id=plane(peer), device_id_type=MESH,
            ).start()
            return carry

        lax.fori_loop(1, 32, step, 0)

    for order, (row, i) in enumerate(lines[:3]):
        whole = recv.at[:, row * 2 + i]
        pltpu.make_async_copy(whole, whole, a_sem.at[order]).wait()
    for chunk in range(CHUNKS):
        span = pl.ds(chunk * QUADS, QUADS)
        arrived = recv.at[span, last]
        pltpu.make_async_copy(arrived, arrived, a_sem.at[3 + chunk]).wait()

        def solve(n, carry):
            quad = chunk * QUADS + n // 2
            r = 2 * (n % 2)
            field = jnp.concatenate([recv_rows[pl.ds(quad * 1024 + r + odd, 256, stride=4), :] for odd in range(2)], 1)
            full = dot_nn(weight3(wx[0], wx[1]), data3(field, 0))
            factor = jnp.concatenate([green_rows[pl.ds(4 * quad + r + odd, 256, stride=32), :] for odd in range(2)], 1)
            product = jnp.concatenate([full[:256] * factor, full[256:] * factor], 0)
            result = dot_nn(weight3(wxi[0], wxi[1]), data3(product, 0))
            for odd in range(2):
                back_rows[pl.ds(quad * 1024 + r + odd, 256, stride=4), :] = result[:, odd * 128 : odd * 128 + 128]
            return carry

        lax.fori_loop(0, 2 * QUADS, solve, 0)
        give_back(0, pl.ds(other * 2, 2), span)
    for i in range(2):
        give_back(1 + i, pl.ds(yh * 2 + i, 1), pl.ds(0, 8))

    loads[6].wait()

    def inverse_yz(line):
        def step(zt, carry):
            columns = []
            for k in range(2):
                blocks = []
                for c in range(2):
                    for xt in range(4):
                        for r in range(4):
                            start = (xt * 8 + zt * 2 + k) * 256 + line * 8 + c * 4 + r
                            blocks.append(home_rows[pl.ds(start, 8, stride=32), :])
                columns.append(jnp.concatenate(blocks, 0))
            along = dot_nn(weight3(wyi[0], wyi[1]), data3(jnp.concatenate(columns, 1), 0))
            field = jnp.concatenate(
                [along[c * 128 : c * 128 + 128, k * 128 : k * 128 + 128] for k in range(2) for c in range(2)], 1
            )
            b[zt] = dot_nt(weight3(wzi[zt, 0], wzi[zt, 1]), data3(field, 1))
            return carry

        lax.fori_loop(0, 4, step, 0)

    def back_to_slabs(i, row):
        for _ in range(1):

            def step(n, carry):
                at = n * 8
                turned = []
                for e in range(2):
                    value = [
                        [b[slots[j], pl.ds(pl.multiple_of(e * 256 + c * 128 + at, 8), 8), :] for c in range(2)]
                        for j in range(4)
                    ]
                    (ar, ai), (br, bi), (cr, ci), (dr, di) = [
                        (value[l][0] + s * value[m][0], value[l][1] + s * value[m][1])
                        for l, m, s in ((0, 2, 1.0), (0, 2, -1.0), (1, 3, 1.0), (1, 3, -1.0))
                    ]
                    sums = [(ar + cr, ai + ci), (br - di, bi + dr), (ar - cr, ai - ci), (br + di, bi - dr)]
                    turned.append(
                        [
                            (re * cos_t[e][k] - im * sin_t[e][k], re * sin_t[e][k] + im * cos_t[e][k])
                            for k, (re, im) in enumerate(sums)
                        ]
                    )
                for k in range(4):
                    part[0, row, i, k, pl.ds(pl.multiple_of(at, 8), 8), :] = turned[0][k][0] + turned[1][k][0]
                    part[1, row, i, k, pl.ds(pl.multiple_of(at, 8), 8), :] = sigma * (turned[0][k][0] - turned[1][k][1])
                return carry

            lax.fori_loop(0, 16, step, 0)

    def sum_copy(i, member):
        slot = (ym - member) % 4 - 1
        return pltpu.make_async_remote_copy(
            part.at[member // 2, member % 2, i], partial.at[slot, i], r_out.at[i], r_sem.at[i, slot],
            device_id=ring(member), device_id_type=MESH,
        )

    def home_line(row, i):
        inverse_yz(row * 2 + i)
        back_to_slabs(i, row)

    def finish(i):
        for step in range(3):
            pltpu.make_async_copy(partial.at[step, i], partial.at[step, i], r_sem.at[i, step]).wait()

        def add(k, carry):
            total[k, i] = (part[yl, yh, i, k] + partial[0, i, k]) + (partial[1, i, k] + partial[2, i, k])
            return carry

        lax.fori_loop(0, 4, add, 0)
        pltpu.make_async_copy(total.at[z, i, pl.ds(core * 64, 64)], final.at[q, i], f_sem.at[i]).start()

        def return_slab(step, carry):
            peer = (q + step) % 8
            pltpu.make_async_remote_copy(
                total.at[peer // 2, i, pl.ds((peer % 2) * 64, 64)], final.at[q, i], f_out.at[i], f_sem.at[i],
                device_id=(yl * 8 + peer, ta), device_id_type=MESH,
            ).start()
            return carry

        lax.fori_loop(1, 8, return_slab, 0)

    both = home.at[:, :, pl.ds(other * 2, 2)]
    pltpu.make_async_copy(both, both, h_sem.at[0]).wait()
    for i in range(2):
        home_line(other, i)
        sum_copy(i, other).start()
        sum_copy(i, 2 + other).start()
    for i in range(2):
        single = home.at[:, :, yh * 2 + i]
        pltpu.make_async_copy(single, single, h_sem.at[1 + i]).wait()
        home_line(yh, i)
        sum_copy(i, (1 - yl) * 2 + yh).start()
        finish(i)
    out_rows = out.reshape(64 * 16, 128)
    for i in range(2):
        pltpu.make_async_copy(final.at[:, i], final.at[:, i], f_sem.at[i]).wait()
        for n in range(8):
            out_rows[pl.ds(2 * n + i, 64, stride=16), :] = final[n, i]

    def drain(ref, sem):
        pltpu.make_async_copy(ref, ref, sem).wait()

    drain(zs.at[pl.ds(0, 14)], z_out)
    for i in range(2):
        drain(raw.at[pl.ds(0, 3), i], y_out.at[i])
    for order in range(4):
        drain(send.at[order, pl.ds(0, 31)], a_out.at[order])
    drain(home.at[pl.ds(0, 31), :, pl.ds(0, 2)], h_out.at[0])
    for i in range(2):
        drain(home.at[pl.ds(0, 31), :, i], h_out.at[1 + i])
        drain(partial.at[:, i], r_out.at[i])
        drain(final.at[pl.ds(0, 7), i], f_out.at[i])


def on_device(consts, charge, green_hat):
    any_spec = pl.BlockSpec(memory_space=pl.ANY)
    vmem_spec = pl.BlockSpec(memory_space=pltpu.VMEM)
    dma = pltpu.SemaphoreType.DMA
    return pl.pallas_call(
        kernel,
        out_shape=jax.ShapeDtypeStruct((64, 16, 128), F32),
        in_specs=[vmem_spec] + [any_spec] * 7,
        out_specs=vmem_spec,
        scratch_shapes=[
            pltpu.VMEM((256, 32, 128), F32),
            pltpu.VMEM((2, 512, 256), BF16),
            pltpu.VMEM((2, 256, 512), BF16),
            pltpu.VMEM((2, 256, 256), BF16),
            pltpu.VMEM((2, 256, 256), BF16),
            pltpu.VMEM((2, 128, 128), F32),
            pltpu.VMEM((8, 8, 128), F32),
            pltpu.VMEM((8, 2, 256, 256), BF16),
            pltpu.VMEM((4, 2, 512, 512), BF16),
            pltpu.VMEM((16, 64, 128), F32),
            pltpu.VMEM((4, 2, 4, 128, 128), F32),
            pltpu.VMEM((4, 2, 2, 256, 128), BF16),
            pltpu.VMEM((4, 32, 8, 8, 128), F32),
            pltpu.VMEM((8, 4, 256, 128), F32),
            pltpu.VMEM((8, 4, 256, 128), F32),
            pltpu.VMEM((32, 8, 4, 8, 128), F32),
            pltpu.VMEM((4, 512, 128), F32),
            pltpu.VMEM((2, 2, 2, 4, 128, 128), F32),
            pltpu.VMEM((3, 2, 4, 128, 128), F32),
            pltpu.VMEM((4, 2, 128, 128), F32),
            pltpu.VMEM((8, 2, 64, 128), F32),
            dma((7,)),
            dma((2,)),
            dma,
            dma((2, 3)),
            dma((2,)),
            dma((3 + CHUNKS,)),
            dma((4,)),
            dma((3,)),
            dma((3,)),
            dma((2, 3)),
            dma((2,)),
            dma((2,)),
            dma((2,)),
        ],
        compiler_params=pltpu.CompilerParams(
            collective_id=0, has_side_effects=True, vmem_limit_bytes=60 * 1024 * 1024
        ),
    )(charge, green_hat, *consts)


def solution(mesh):
    consts = tables()
    return jax.shard_map(
        functools.partial(on_device, consts),
        mesh=mesh,
        in_specs=(P("gz", "ta", None), P(None, "ta", "gz")),
        out_specs=P("gz", "ta", None),
        check_vma=False,
    )
```

```python
import functools

import jax
import jax.numpy as jnp
import ml_dtypes
import numpy as np
from jax import lax
from jax.experimental import pallas as pl
from jax.experimental.pallas import tpu as pltpu
from jax.sharding import PartitionSpec as P

MESH = pl.DeviceIdType.MESH
F32 = jnp.float32
BF16 = jnp.bfloat16
SHARES = ((0, 3), (3, 2), (5, 2), (7, 1))


def halves(table):
    high = table.astype(ml_dtypes.bfloat16)
    low = (table - high.astype(np.float64)).astype(ml_dtypes.bfloat16)
    return np.stack([high, low])


def tables():
    peer = np.arange(32)
    row = np.arange(4)
    x_of = ((peer // 8) * 16 + (peer % 8) * 2)[None, :] + ((row // 2) * 64 + row % 2)[:, None]
    kx = np.arange(256)
    angle = 2 * np.pi / 256 * (kx[:, None, None] * x_of[None] % 256)
    cosine, sine = np.cos(angle), np.sin(angle)
    wx = np.stack([np.stack([cosine, sine], 3), np.stack([-sine, cosine], 3)]).reshape(512, 256)
    y = np.arange(128)
    wy = []
    for y_half in range(2):
        ky = 128 * y_half + np.arange(128).reshape(4, 8, 4).transpose(0, 2, 1).reshape(128)
        angle = 2 * np.pi / 256 * (ky[:, None] * y[None] % 256)
        cosine, sine = np.cos(angle), np.sin(angle)
        wy.append(np.block([[cosine, sine], [-sine, cosine]]))
    wy = np.stack(wy)
    v = np.arange(128)
    low_bits = np.concatenate([2 * np.arange(64), 2 * np.arange(64) + 1])
    angle = 2 * np.pi / 128 * (low_bits[:, None] * v[None] % 128)
    alpha = np.stack([np.cos(angle), np.sin(angle)]).astype(np.float32)
    reverse = np.array([0, 2, 1, 3])
    s = 4 * reverse[None, :, None] + 2 * np.arange(2)[:, None, None] + np.arange(2)[None, None]
    angle = 2 * np.pi / 2048 * (s.reshape(2, 8)[..., None] * v % 2048)
    beta = np.stack([np.cos(angle), np.sin(angle)], 2).astype(np.float32)
    beta = np.pad(beta, ((0, 0), (0, 0), (0, 6), (0, 0)))
    return (
        halves(wx),
        halves(wx.T * 2.0**-27),
        np.stack([halves(w) for w in wy]),
        np.stack([halves(w.T) for w in wy]),
        alpha,
        beta,
    )


def split(value):
    high = value.astype(BF16)
    return high, (value - high.astype(F32)).astype(BF16)


def weight3(high, low):
    return jnp.concatenate([high, high, low], axis=1)


def data3(value, axis):
    high, low = split(value)
    return jnp.concatenate([high, low, high], axis=axis)


def dot_nn(weight, data):
    return jnp.dot(weight, data, preferred_element_type=F32)


def dot_nt(weight, data):
    return lax.dot_general(weight, data, (((1,), (1,)), ((), ())), preferred_element_type=F32)


def kernel(
    charge, green, wx_hbm, wxi_hbm, wy_hbm, wyi_hbm, alpha_hbm, beta_hbm,
    out,
    g, wx, wxi, wy, wyi, alpha, beta, wz, wzi, zs, raw, a, send, recv, back, home, b, part, partial, total, final,
    load_sem, z_sem, z_out, y_sem, y_out, a_sem, a_out, h_sem, h_out, r_sem, r_out, f_sem, f_out, extra, x_sem, x_out,
):
    gz = lax.axis_index("gz")
    ta = lax.axis_index("ta")
    yl, q = gz // 8, gz % 8
    z, core = q // 2, q % 2
    yh, xc = ta // 4, ta % 4
    ym = yl * 2 + yh
    me = xc * 8 + q

    def plane(peer):
        return (yl * 8 + peer % 8, yh * 4 + peer // 8)

    def ring(member):
        return ((member // 2) * 8 + q, (member % 2) * 4 + xc)

    def across(peer):
        return ((1 - yl) * 8 + peer, ta)

    loads = [
        pltpu.make_async_copy(alpha_hbm, alpha, load_sem.at[0]),
        pltpu.make_async_copy(beta_hbm.at[yl], beta, load_sem.at[1]),
        pltpu.make_async_copy(wy_hbm.at[yh], wy, load_sem.at[2]),
        pltpu.make_async_copy(wx_hbm, wx, load_sem.at[3]),
        pltpu.make_async_copy(green, g, load_sem.at[4]),
        pltpu.make_async_copy(wxi_hbm, wxi, load_sem.at[5]),
        pltpu.make_async_copy(wyi_hbm.at[yh], wyi, load_sem.at[6]),
    ]
    for load in loads:
        load.start()

    barrier = pltpu.get_barrier_semaphore()

    def greet(step, carry):
        pl.semaphore_signal(barrier, inc=1, device_id=plane((me + step) % 32), device_id_type=MESH)
        return carry

    lax.fori_loop(1, 32, greet, 0)
    for step in range(1, 4):
        pl.semaphore_signal(barrier, inc=1, device_id=ring((ym + step) % 4), device_id_type=MESH)

    def greet_across(step, carry):
        pl.semaphore_signal(barrier, inc=1, device_id=across((q + step) % 8), device_id_type=MESH)
        return carry

    lax.fori_loop(1, 8, greet_across, 0)
    rows = charge.reshape(64 * 16, 128)
    for x in range(16):
        zs[x] = rows[pl.ds(x, 64, stride=16), :]
    pl.semaphore_wait(barrier, 41)

    for i in range(2):
        keep = pltpu.make_async_copy(
            zs.at[2 * q + i], raw.at[ym, i, z, pl.ds(core * 64, 64)], z_sem.at[i]
        )
        keep.start()

        if i == 0:

            def spread_across(step, carry):
                peer = (q + step) % 8
                pltpu.make_async_remote_copy(
                    zs.at[2 * peer], raw.at[ym, 0, z, pl.ds(core * 64, 64)], y_out.at[0], y_sem.at[0, 1],
                    device_id=across(peer), device_id_type=MESH,
                ).start()
                return carry

            lax.fori_loop(0, 8, spread_across, 0)

        def spread(step, carry):
            peer = (q + step) % 8
            pltpu.make_async_remote_copy(
                zs.at[2 * peer + i], raw.at[ym, i, z, pl.ds(core * 64, 64)], z_out, z_sem.at[i],
                device_id=(yl * 8 + peer, ta), device_id_type=MESH,
            ).start()
            return carry

        lax.fori_loop(1, 8, spread, 0)

    loads[0].wait()
    loads[1].wait()

    def build(slot, carry):
        turn = beta[slot]
        cos_b, sin_b = turn[0:1], turn[1:2]
        cos_a, sin_a = alpha[0], alpha[1]
        cosine = cos_a * cos_b - sin_a * sin_b
        sine = sin_a * cos_b + cos_a * sin_b
        blocks = []
        for k in range(2):
            c_k, s_k = cosine[k * 64 : k * 64 + 64], sine[k * 64 : k * 64 + 64]
            blocks += [jnp.concatenate([c_k, s_k], 1), jnp.concatenate([-s_k, c_k], 1)]
        table = jnp.concatenate(blocks, 0)
        high, low = split(table)
        wz[slot, 0] = high
        wz[slot, 1] = low
        high, low = split(table.T)
        wzi[slot, 0] = high
        wzi[slot, 1] = low
        return carry

    lax.fori_loop(0, 8, build, 0)

    def ring_copy(i, step):
        return pltpu.make_async_remote_copy(
            raw.at[ym, i], raw.at[ym, i], y_out.at[i], y_sem.at[i, step - 1],
            device_id=ring((ym + step) % 4), device_id_type=MESH,
        )

    for i in range(2):
        pltpu.make_async_copy(raw.at[ym, i], raw.at[ym, i], z_sem.at[i]).wait()
        if i == 1:
            ring_copy(i, 2).start()
    for i in range(2):
        for step in (1, 3):
            ring_copy(i, step).start()

    first = yl == 0
    sigma = jnp.where(first, 1.0, -1.0).astype(F32)

    def pick(zero, one):
        return jnp.where(first, np.float32(zero), np.float32(one))

    cos_t = [[pick(np.cos(np.pi * (e) * n / 8), np.cos(np.pi * (2 + e) * n / 8)) for n in range(4)] for e in range(2)]
    sin_t = [[pick(np.sin(np.pi * (e) * n / 8), np.sin(np.pi * (2 + e) * n / 8)) for n in range(4)] for e in range(2)]
    slots = (0, 2, 1, 3)

    def over_slabs(row, i):
        for _ in range(1):

            def step(n, carry):
                at = pl.multiple_of(n * 16, 16)
                near = [raw[row, i, k, pl.ds(at, 16), :] for k in range(4)]
                far = [raw[2 + row, i, k, pl.ds(at, 16), :] for k in range(4)]
                for e in range(2):
                    re, im = [], []
                    for k in range(4):
                        ct, st = cos_t[e][k], sin_t[e][k]
                        if e == 0:
                            u = near[k] + sigma * far[k]
                            re.append(u * ct if k else u)
                            im.append(-(u * st) if k else jnp.zeros_like(u))
                        else:
                            w = sigma * far[k]
                            re.append(near[k] * ct - w * st if k else near[k])
                            im.append(-(near[k] * st + w * ct) if k else -w)
                    ar, ai = re[0] + re[2], im[0] + im[2]
                    br, bi = re[0] - re[2], im[0] - im[2]
                    cr, ci = re[1] + re[3], im[1] + im[3]
                    dr, di = re[1] - re[3], im[1] - im[3]
                    sums = [(ar + cr, ai + ci), (br + di, bi - dr), (ar - cr, ai - ci), (br - di, bi + dr)]
                    for j in range(4):
                        for c in range(2):
                            high, low = split(sums[j][c])
                            spot = pl.ds(pl.multiple_of(c * 128 + at, 16), 16)
                            a[slots[j], e, 0, spot, :] = high
                            a[slots[j], e, 1, spot, :] = low
                return carry

            lax.fori_loop(0, 8, step, 0)

    send_rows = send.reshape(4 * 32 * 64, 128)
    home_rows = home.reshape(32 * 256, 128)
    mine = pl.ds(pl.multiple_of(me * 8, 8), 8)

    def partner(step):
        turn = step // 2
        return ((xc + turn) % 4) * 8 + ((z + turn // 4 + turn) % 4) * 2 + (core + step) % 2


    def plane_copy(line, peer, span, slot, sem):
        return pltpu.make_async_remote_copy(
            send.at[line, peer, span], recv.at[span, line, mine], a_out.at[slot], sem,
            device_id=plane(peer), device_id_type=MESH,
        )

    def plane_keep(line, span, sem):
        pltpu.make_async_copy(send.at[line, me, span], recv.at[span, line, mine], sem).start()

    def send_first(line, zt, here):
        def step(n, carry):
            peer = ((xc + n // 2) % 4) * 8 + zt * 2 + (core + n) % 2
            keep = jnp.logical_and(here, n == 0)

            @pl.when(keep)
            def _():
                plane_keep(line, pl.ds(0, 8), a_sem.at[0])

            @pl.when(jnp.logical_not(keep))
            def _():
                plane_copy(line, peer, pl.ds(0, 8), 0, a_sem.at[0]).start()

            return carry

        lax.fori_loop(0, 8, step, 0)

    def send_line(order, line, span, sem):
        plane_keep(line, span, sem)

        def step(n, carry):
            plane_copy(line, partner(n), span, order, sem).start()
            return carry

        lax.fori_loop(1, 32, step, 0)

    def far_first(n):
        return (z + jnp.where(n == 0, 2, jnp.where(n == 1, 1, jnp.where(n == 2, 3, 0)))) % 4

    def forward_zy(order, line):
        def step(n, carry):
            zt = far_first(n)
            outs = []
            for e in range(2):
                weight = weight3(wz[zt * 2 + e, 0], wz[zt * 2 + e, 1])
                high, low = a[zt, e, 0], a[zt, e, 1]
                outs.append(dot_nn(weight, jnp.concatenate([high, low, high], 0)))
            field = jnp.concatenate(
                [
                    jnp.concatenate([outs[e][k * 128 : k * 128 + 64], outs[e][k * 128 + 64 : k * 128 + 128]], 1)
                    for k in range(2)
                    for e in range(2)
                ],
                0,
            )
            plane_out = dot_nt(weight3(wy[0], wy[1]), data3(field, 1))
            for c in range(2):
                for xt in range(4):
                    for r in range(4):
                        at = c * 128 + xt * 32 + r * 8
                        for k in range(2):
                            start = (line * 32 + xt * 8 + zt * 2 + k) * 64 + c * 4 + r
                            send_rows[pl.ds(start, 8, stride=8), :] = plane_out[at : at + 8, k * 128 : k * 128 + 128]
            if order == 0:
                send_first(line, zt, n == 3)

            return carry

        lax.fori_loop(0, 4, step, 0)
        if 0 < order < 3:
            send_line(order, line, pl.ds(0, 8), a_sem.at[order])

    loads[2].wait()
    other = 1 - yh
    lines = ((yh, 0), (yh, 1), (other, 0), (other, 1))
    for order, (row, i) in enumerate(lines):
        for step in ((2,) if order < 2 else (1, 3)):
            source = (ym - step) % 4
            pltpu.make_async_copy(raw.at[source, i], raw.at[source, i], y_sem.at[i, step - 1]).wait()
        over_slabs(row, i)
        forward_zy(order, row * 2 + i)

    last = other * 2 + 1
    for share, (begin, size) in enumerate(SHARES):
        send_line(3, last, pl.ds(begin, size), a_sem.at[3 + share])

    loads[3].wait()
    loads[4].wait()
    loads[5].wait()
    green_rows = g.reshape(256 * 32, 128)
    recv_rows = recv.reshape(8 * 1024, 128)
    back_rows = back.reshape(8 * 1024, 128)

    def give_back(slot, lines_of, span):
        pltpu.make_async_copy(back.at[span, lines_of, mine], home.at[me, span, lines_of], h_sem.at[slot]).start()

        def step(n, carry):
            peer = partner(n)
            pltpu.make_async_remote_copy(
                back.at[span, lines_of, pl.ds(pl.multiple_of(peer * 8, 8), 8)], home.at[me, span, lines_of],
                h_out.at[slot], h_sem.at[slot], device_id=plane(peer), device_id_type=MESH,
            ).start()
            return carry

        lax.fori_loop(1, 32, step, 0)

    for order, (row, i) in enumerate(lines[:3]):
        whole = recv.at[:, row * 2 + i]
        pltpu.make_async_copy(whole, whole, a_sem.at[order]).wait()
    for share, (begin, size) in enumerate(SHARES):
        span = pl.ds(begin, size)
        arrived = recv.at[span, last]
        pltpu.make_async_copy(arrived, arrived, a_sem.at[3 + share]).wait()

        def solve(n, carry):
            quad = begin + n // 2
            r = 2 * (n % 2)
            field = jnp.concatenate([recv_rows[pl.ds(quad * 1024 + r + odd, 256, stride=4), :] for odd in range(2)], 1)
            full = dot_nn(weight3(wx[0], wx[1]), data3(field, 0))
            factor = jnp.concatenate([green_rows[pl.ds(4 * quad + r + odd, 256, stride=32), :] for odd in range(2)], 1)
            product = jnp.concatenate([full[:256] * factor, full[256:] * factor], 0)
            result = dot_nn(weight3(wxi[0], wxi[1]), data3(product, 0))
            for odd in range(2):
                back_rows[pl.ds(quad * 1024 + r + odd, 256, stride=4), :] = result[:, odd * 128 : odd * 128 + 128]
            return carry

        lax.fori_loop(0, 2 * size, solve, 0)
        give_back(0, pl.ds(other * 2, 2), span)
    for i in range(2):
        give_back(1 + i, pl.ds(yh * 2 + i, 1), pl.ds(0, 8))

    loads[6].wait()

    def inverse_yz(line):
        def step(zt, carry):
            columns = []
            for k in range(2):
                blocks = []
                for c in range(2):
                    for xt in range(4):
                        for r in range(4):
                            start = (xt * 8 + zt * 2 + k) * 256 + line * 8 + c * 4 + r
                            blocks.append(home_rows[pl.ds(start, 8, stride=32), :])
                columns.append(jnp.concatenate(blocks, 0))
            along = dot_nn(weight3(wyi[0], wyi[1]), data3(jnp.concatenate(columns, 1), 0))
            lower = lax.broadcasted_iota(jnp.int32, (128, 128), 1) < 64
            fields = [[], []]
            for k in range(2):
                re, im = [along[c * 128 : c * 128 + 128, k * 128 : k * 128 + 128] for c in range(2)]
                fields[0].append(jnp.where(lower, re, pltpu.roll(im, 64, 1)))
                fields[1].append(jnp.where(lower, pltpu.roll(re, 64, 1), im))
            for e in range(2):
                weight = weight3(wzi[zt * 2 + e, 0], wzi[zt * 2 + e, 1])
                b[zt, e * 256 : e * 256 + 256, :] = dot_nt(weight, data3(jnp.concatenate(fields[e], 1), 1))
            return carry

        lax.fori_loop(0, 4, step, 0)

    def back_to_slabs(i, row):
        for _ in range(1):

            def step(n, carry):
                at = n * 8
                turned = []
                for e in range(2):
                    value = [
                        [b[slots[j], pl.ds(pl.multiple_of(e * 256 + c * 128 + at, 8), 8), :] for c in range(2)]
                        for j in range(4)
                    ]
                    (ar, ai), (br, bi), (cr, ci), (dr, di) = [
                        (value[l][0] + s * value[m][0], value[l][1] + s * value[m][1])
                        for l, m, s in ((0, 2, 1.0), (0, 2, -1.0), (1, 3, 1.0), (1, 3, -1.0))
                    ]
                    sums = [(ar + cr, ai + ci), (br - di, bi + dr), (ar - cr, ai - ci), (br + di, bi - dr)]
                    turned.append(
                        [
                            (re * cos_t[e][k] - im * sin_t[e][k], re * sin_t[e][k] + im * cos_t[e][k])
                            for k, (re, im) in enumerate(sums)
                        ]
                    )
                for k in range(4):
                    part[0, row, i, k, pl.ds(pl.multiple_of(at, 8), 8), :] = turned[0][k][0] + turned[1][k][0]
                    part[1, row, i, k, pl.ds(pl.multiple_of(at, 8), 8), :] = sigma * (turned[0][k][0] - turned[1][k][1])
                return carry

            lax.fori_loop(0, 16, step, 0)

    def sum_copy(i, member):
        slot = (ym - member) % 4 - 1
        return pltpu.make_async_remote_copy(
            part.at[member // 2, member % 2, i], partial.at[slot, i], r_out.at[i], r_sem.at[i, slot],
            device_id=ring(member), device_id_type=MESH,
        )

    def home_line(row, i):
        inverse_yz(row * 2 + i)
        back_to_slabs(i, row)

    def finish(i):
        for slot in (0, 1, 2) if i == 0 else (0, 2):
            pltpu.make_async_copy(partial.at[slot, i], partial.at[slot, i], r_sem.at[i, slot]).wait()

        def add(k, carry):
            value = part[yl, yh, i, k] + partial[0, i, k] + partial[2, i, k]
            total[k, i] = value + partial[1, i, k] if i == 0 else value
            return carry

        lax.fori_loop(0, 4, add, 0)
        pltpu.make_async_copy(total.at[z, i, pl.ds(core * 64, 64)], final.at[q, i], f_sem.at[i]).start()

        def return_slab(step, carry):
            peer = (q + step) % 8
            pltpu.make_async_remote_copy(
                total.at[peer // 2, i, pl.ds((peer % 2) * 64, 64)], final.at[q, i], f_out.at[i], f_sem.at[i],
                device_id=(yl * 8 + peer, ta), device_id_type=MESH,
            ).start()
            return carry

        lax.fori_loop(1, 8, return_slab, 0)

    def return_across(step, carry):
        peer = (q + step) % 8
        pltpu.make_async_remote_copy(
            part.at[1 - yl, yh, 1, peer // 2, pl.ds((peer % 2) * 64, 64)], extra.at[q], x_out, x_sem,
            device_id=across(peer), device_id_type=MESH,
        ).start()
        return carry

    both = home.at[:, :, pl.ds(other * 2, 2)]
    pltpu.make_async_copy(both, both, h_sem.at[0]).wait()
    for i in range(2):
        home_line(other, i)
        sum_copy(i, other).start()
        sum_copy(i, 2 + other).start()
    for i in range(2):
        single = home.at[:, :, yh * 2 + i]
        pltpu.make_async_copy(single, single, h_sem.at[1 + i]).wait()
        home_line(yh, i)
        if i == 0:
            sum_copy(i, (1 - yl) * 2 + yh).start()
        else:
            lax.fori_loop(0, 8, return_across, 0)
        finish(i)
    out_rows = out.reshape(64 * 16, 128)
    for i in range(2):
        pltpu.make_async_copy(final.at[:, i], final.at[:, i], f_sem.at[i]).wait()
        if i == 1:
            pltpu.make_async_copy(extra, extra, x_sem).wait()
        for n in range(8):
            out_rows[pl.ds(2 * n + i, 64, stride=16), :] = final[n, i] + extra[n] if i else final[n, i]

    def drain(ref, sem):
        pltpu.make_async_copy(ref, ref, sem).wait()

    drain(zs.at[pl.ds(0, 14)], z_out)
    for i in range(2):
        drain(raw.at[pl.ds(0, 3), i], y_out.at[i])
    for order in range(4):
        drain(send.at[order, pl.ds(0, 31)], a_out.at[order])
    drain(home.at[pl.ds(0, 31), :, pl.ds(0, 2)], h_out.at[0])
    for i in range(2):
        drain(home.at[pl.ds(0, 31), :, i], h_out.at[1 + i])
        drain(partial.at[pl.ds(0, 3 - i), i], r_out.at[i])
        drain(final.at[pl.ds(0, 7), i], f_out.at[i])
    drain(extra, x_out)


def on_device(consts, charge, green_hat):
    any_spec = pl.BlockSpec(memory_space=pl.ANY)
    vmem_spec = pl.BlockSpec(memory_space=pltpu.VMEM)
    dma = pltpu.SemaphoreType.DMA
    return pl.pallas_call(
        kernel,
        out_shape=jax.ShapeDtypeStruct((64, 16, 128), F32),
        in_specs=[vmem_spec] + [any_spec] * 7,
        out_specs=vmem_spec,
        scratch_shapes=[
            pltpu.VMEM((256, 32, 128), F32),
            pltpu.VMEM((2, 512, 256), BF16),
            pltpu.VMEM((2, 256, 512), BF16),
            pltpu.VMEM((2, 256, 256), BF16),
            pltpu.VMEM((2, 256, 256), BF16),
            pltpu.VMEM((2, 128, 128), F32),
            pltpu.VMEM((8, 8, 128), F32),
            pltpu.VMEM((8, 2, 256, 256), BF16),
            pltpu.VMEM((8, 2, 256, 256), BF16),
            pltpu.VMEM((16, 64, 128), F32),
            pltpu.VMEM((4, 2, 4, 128, 128), F32),
            pltpu.VMEM((4, 2, 2, 256, 128), BF16),
            pltpu.VMEM((4, 32, 8, 8, 128), F32),
            pltpu.VMEM((8, 4, 256, 128), F32),
            pltpu.VMEM((8, 4, 256, 128), F32),
            pltpu.VMEM((32, 8, 4, 8, 128), F32),
            pltpu.VMEM((4, 512, 128), F32),
            pltpu.VMEM((2, 2, 2, 4, 128, 128), F32),
            pltpu.VMEM((3, 2, 4, 128, 128), F32),
            pltpu.VMEM((4, 2, 128, 128), F32),
            pltpu.VMEM((8, 2, 64, 128), F32),
            dma((7,)),
            dma((2,)),
            dma,
            dma((2, 3)),
            dma((2,)),
            dma((3 + len(SHARES),)),
            dma((4,)),
            dma((3,)),
            dma((3,)),
            dma((2, 3)),
            dma((2,)),
            dma((2,)),
            dma((2,)),
            pltpu.VMEM((8, 64, 128), F32),
            dma,
            dma,
        ],
        compiler_params=pltpu.CompilerParams(
            collective_id=0, has_side_effects=True, vmem_limit_bytes=60 * 1024 * 1024
        ),
    )(charge, green_hat, *consts)


def solution(mesh):
    consts = tables()
    return jax.shard_map(
        functools.partial(on_device, consts),
        mesh=mesh,
        in_specs=(P("gz", "ta", None), P(None, "ta", "gz")),
        out_specs=P("gz", "ta", None),
        check_vma=False,
    )
```

```python
import functools

import jax
import jax.numpy as jnp
import ml_dtypes
import numpy as np
from jax import lax
from jax.experimental import pallas as pl
from jax.experimental.pallas import tpu as pltpu
from jax.sharding import PartitionSpec as P

MESH = pl.DeviceIdType.MESH
F32 = jnp.float32
BF16 = jnp.bfloat16
SHARES = ((0, 3), (3, 3), (6, 2))


def halves(table):
    high = table.astype(ml_dtypes.bfloat16)
    low = (table - high.astype(np.float64)).astype(ml_dtypes.bfloat16)
    return np.stack([high, low])


def tables():
    peer = np.arange(32)
    row = np.arange(4)
    x_of = ((peer // 8) * 16 + (peer % 8) * 2)[None, :] + ((row // 2) * 64 + row % 2)[:, None]
    kx = np.arange(256)
    angle = 2 * np.pi / 256 * (kx[:, None, None] * x_of[None] % 256)
    cosine, sine = np.cos(angle), np.sin(angle)
    wx = np.stack([np.stack([cosine, sine], 3), np.stack([-sine, cosine], 3)]).reshape(512, 256)
    y = np.arange(128)
    wy = []
    for y_half in range(2):
        ky = 128 * y_half + np.arange(128).reshape(4, 8, 4).transpose(0, 2, 1).reshape(128)
        angle = 2 * np.pi / 256 * (ky[:, None] * y[None] % 256)
        cosine, sine = np.cos(angle), np.sin(angle)
        wy.append(np.block([[cosine, sine], [-sine, cosine]]))
    wy = np.stack(wy)
    v = np.arange(128)
    low_bits = np.concatenate([2 * np.arange(64), 2 * np.arange(64) + 1])
    angle = 2 * np.pi / 128 * (low_bits[:, None] * v[None] % 128)
    alpha = np.stack([np.cos(angle), np.sin(angle)]).astype(np.float32)
    reverse = np.array([0, 2, 1, 3])
    s = 4 * reverse[None, :, None] + 2 * np.arange(2)[:, None, None] + np.arange(2)[None, None]
    angle = 2 * np.pi / 2048 * (s.reshape(2, 8)[..., None] * v % 2048)
    beta = np.stack([np.cos(angle), np.sin(angle)], 2).astype(np.float32)
    beta = np.pad(beta, ((0, 0), (0, 0), (0, 6), (0, 0)))
    return (
        halves(wx),
        halves(wx.T * 2.0**-27),
        np.stack([halves(w) for w in wy]),
        np.stack([halves(w.T) for w in wy]),
        alpha,
        beta,
    )


def split(value):
    high = value.astype(BF16)
    return high, (value - high.astype(F32)).astype(BF16)


def weight3(high, low):
    return jnp.concatenate([high, high, low], axis=1)


def data3(value, axis):
    high, low = split(value)
    return jnp.concatenate([high, low, high], axis=axis)


def dot_nn(weight, data):
    return jnp.dot(weight, data, preferred_element_type=F32)


def dot_nt(weight, data):
    return lax.dot_general(weight, data, (((1,), (1,)), ((), ())), preferred_element_type=F32)


def kernel(
    charge, green, wx_hbm, wxi_hbm, wy_hbm, wyi_hbm, alpha_hbm, beta_hbm,
    out,
    g, wx, wxi, wy, wyi, alpha, beta, wz, wzi, zs, raw, a, send, recv, back, home, b, part, partial, total, final,
    load_sem, z_sem, z_out, y_sem, y_out, a_sem, a_out, h_sem, h_out, r_sem, r_out, f_sem, f_out, extra, x_sem, x_out,
):
    gz = lax.axis_index("gz")
    ta = lax.axis_index("ta")
    yl, q = gz >> 3, gz & 7
    z, core = q >> 1, q & 1
    yh, xc = ta >> 2, ta & 3
    ym = yl * 2 + yh
    me = xc * 8 + q

    def plane(peer):
        return (yl * 8 + (peer & 7), yh * 4 + (peer >> 3))

    def ring(member):
        return ((member >> 1) * 8 + q, (member & 1) * 4 + xc)

    def across(peer):
        return ((1 - yl) * 8 + peer, ta)

    loads = [
        pltpu.make_async_copy(alpha_hbm, alpha, load_sem.at[0]),
        pltpu.make_async_copy(beta_hbm.at[yl], beta, load_sem.at[1]),
        pltpu.make_async_copy(wy_hbm.at[yh], wy, load_sem.at[2]),
        pltpu.make_async_copy(wx_hbm, wx, load_sem.at[3]),
        pltpu.make_async_copy(green, g, load_sem.at[4]),
        pltpu.make_async_copy(wxi_hbm, wxi, load_sem.at[5]),
        pltpu.make_async_copy(wyi_hbm.at[yh], wyi, load_sem.at[6]),
    ]
    for load in loads:
        load.start()

    barrier = pltpu.get_barrier_semaphore()

    def greet(step, carry):
        pl.semaphore_signal(barrier, inc=1, device_id=plane((me + step) & 31), device_id_type=MESH)
        return carry

    lax.fori_loop(1, 32, greet, 0)
    for step in range(1, 4):
        pl.semaphore_signal(barrier, inc=1, device_id=ring((ym + step) & 3), device_id_type=MESH)

    def greet_across(step, carry):
        pl.semaphore_signal(barrier, inc=1, device_id=across((q + step) & 7), device_id_type=MESH)
        return carry

    lax.fori_loop(1, 8, greet_across, 0)
    rows = charge.reshape(64 * 16, 128)
    for x in range(16):
        zs[x] = rows[pl.ds(x, 64, stride=16), :]
    pl.semaphore_wait(barrier, 41)

    for i in range(2):
        keep = pltpu.make_async_copy(
            zs.at[2 * q + i], raw.at[ym, i, z, pl.ds(core * 64, 64)], z_sem.at[i]
        )
        keep.start()

        if i == 0:

            def spread_across(step, carry):
                peer = (q + step) & 7
                pltpu.make_async_remote_copy(
                    zs.at[2 * peer], raw.at[ym, 0, z, pl.ds(core * 64, 64)], y_out.at[0], y_sem.at[0, 1],
                    device_id=across(peer), device_id_type=MESH,
                ).start()
                return carry

            lax.fori_loop(0, 8, spread_across, 0)

        def spread(step, carry):
            peer = (q + step) & 7
            pltpu.make_async_remote_copy(
                zs.at[2 * peer + i], raw.at[ym, i, z, pl.ds(core * 64, 64)], z_out, z_sem.at[i],
                device_id=(yl * 8 + peer, ta), device_id_type=MESH,
            ).start()
            return carry

        lax.fori_loop(1, 8, spread, 0)

    loads[0].wait()
    loads[1].wait()

    def build(slot, carry):
        turn = beta[slot]
        cos_b, sin_b = turn[0:1], turn[1:2]
        cos_a, sin_a = alpha[0], alpha[1]
        cosine = cos_a * cos_b - sin_a * sin_b
        sine = sin_a * cos_b + cos_a * sin_b
        blocks = []
        for k in range(2):
            c_k, s_k = cosine[k * 64 : k * 64 + 64], sine[k * 64 : k * 64 + 64]
            blocks += [jnp.concatenate([c_k, s_k], 1), jnp.concatenate([-s_k, c_k], 1)]
        table = jnp.concatenate(blocks, 0)
        high, low = split(table)
        wz[slot, 0] = high
        wz[slot, 1] = low
        high, low = split(table.T)
        wzi[slot, 0] = high
        wzi[slot, 1] = low
        return carry

    lax.fori_loop(0, 8, build, 0)

    def ring_copy(i, step):
        return pltpu.make_async_remote_copy(
            raw.at[ym, i], raw.at[ym, i], y_out.at[i], y_sem.at[i, step - 1],
            device_id=ring((ym + step) & 3), device_id_type=MESH,
        )

    for i in range(2):
        pltpu.make_async_copy(raw.at[ym, i], raw.at[ym, i], z_sem.at[i]).wait()
        if i == 1:
            ring_copy(i, 2).start()
    for i in range(2):
        for step in (1, 3):
            ring_copy(i, step).start()

    first = yl == 0
    sigma = jnp.where(first, 1.0, -1.0).astype(F32)

    def pick(zero, one):
        return jnp.where(first, np.float32(zero), np.float32(one))

    cos_t = [[pick(np.cos(np.pi * (e) * n / 8), np.cos(np.pi * (2 + e) * n / 8)) for n in range(4)] for e in range(2)]
    sin_t = [[pick(np.sin(np.pi * (e) * n / 8), np.sin(np.pi * (2 + e) * n / 8)) for n in range(4)] for e in range(2)]
    slots = (0, 2, 1, 3)

    def over_slabs(row, i):
        for _ in range(1):

            def step(n, carry):
                at = pl.multiple_of(n * 16, 16)
                near = [raw[row, i, k, pl.ds(at, 16), :] for k in range(4)]
                far = [raw[2 + row, i, k, pl.ds(at, 16), :] for k in range(4)]
                for e in range(2):
                    re, im = [], []
                    for k in range(4):
                        ct, st = cos_t[e][k], sin_t[e][k]
                        if e == 0:
                            u = near[k] + sigma * far[k]
                            re.append(u * ct if k else u)
                            im.append(-(u * st) if k else jnp.zeros_like(u))
                        else:
                            w = sigma * far[k]
                            re.append(near[k] * ct - w * st if k else near[k])
                            im.append(-(near[k] * st + w * ct) if k else -w)
                    ar, ai = re[0] + re[2], im[0] + im[2]
                    br, bi = re[0] - re[2], im[0] - im[2]
                    cr, ci = re[1] + re[3], im[1] + im[3]
                    dr, di = re[1] - re[3], im[1] - im[3]
                    sums = [(ar + cr, ai + ci), (br + di, bi - dr), (ar - cr, ai - ci), (br - di, bi + dr)]
                    for j in range(4):
                        for c in range(2):
                            high, low = split(sums[j][c])
                            spot = pl.ds(pl.multiple_of(c * 128 + at, 16), 16)
                            a[slots[j], e, 0, spot, :] = high
                            a[slots[j], e, 1, spot, :] = low
                return carry

            lax.fori_loop(0, 8, step, 0)

    send_rows = send.reshape(32 * 256, 128)
    home_rows = home.reshape(32 * 256, 128)
    mine = pl.ds(pl.multiple_of(me * 8, 8), 8)

    def partner(step):
        turn = step >> 1
        xt = (xc + turn) & 3
        zc = (((z + (turn >> 2) + turn) & 3) << 1) + ((core + step) & 1)
        return (xt << 3) + zc, (yl * 8 + zc, yh * 4 + xt)

    def send_lines(lines_of, span, out_sem, sem):
        pltpu.make_async_copy(send.at[me, span, lines_of], recv.at[span, lines_of, mine], sem).start()

        def step(n, carry):
            peer, place = partner(n)
            pltpu.make_async_remote_copy(
                send.at[peer, span, lines_of], recv.at[span, lines_of, mine], out_sem, sem,
                device_id=place, device_id_type=MESH,
            ).start()
            return carry

        lax.fori_loop(1, 32, step, 0)

    def forward_zy(order, line):
        def step(n, carry):
            zt = n
            outs = []
            for e in range(2):
                weight = weight3(wz[zt * 2 + e, 0], wz[zt * 2 + e, 1])
                high, low = a[zt, e, 0], a[zt, e, 1]
                outs.append(dot_nn(weight, jnp.concatenate([high, low, high], 0)))
            field = jnp.concatenate(
                [
                    jnp.concatenate([outs[e][k * 128 : k * 128 + 64], outs[e][k * 128 + 64 : k * 128 + 128]], 1)
                    for k in range(2)
                    for e in range(2)
                ],
                0,
            )
            plane_out = dot_nt(weight3(wy[0], wy[1]), data3(field, 1))
            for c in range(2):
                for xt in range(4):
                    for r in range(4):
                        at = c * 128 + xt * 32 + r * 8
                        for k in range(2):
                            start = (xt * 8 + zt * 2 + k) * 256 + line * 8 + c * 4 + r
                            send_rows[pl.ds(start, 8, stride=32), :] = plane_out[at : at + 8, k * 128 : k * 128 + 128]

            return carry

        lax.fori_loop(0, 4, step, 0)
        if order < 2:
            for begin in (0, 4):
                send_lines(pl.ds(line, 1), pl.ds(begin, 4), a_out.at[order], a_sem.at[order])

    loads[2].wait()
    other = 1 - yh
    lines = ((yh, 0), (yh, 1), (other, 0), (other, 1))
    for order, (row, i) in enumerate(lines):
        for step in ((2,) if order < 2 else (1, 3)):
            source = (ym - step) & 3
            pltpu.make_async_copy(raw.at[source, i], raw.at[source, i], y_sem.at[i, step - 1]).wait()
        over_slabs(row, i)
        forward_zy(order, row * 2 + i)

    late = pl.ds(other * 2, 2)
    for share, (begin, size) in enumerate(SHARES):
        send_lines(late, pl.ds(begin, size), a_out.at[2], a_sem.at[2 + share])

    loads[3].wait()
    loads[4].wait()
    loads[5].wait()
    green_rows = g.reshape(256 * 32, 128)
    recv_rows = recv.reshape(8 * 1024, 128)
    back_rows = back.reshape(8 * 1024, 128)

    def give_back(slot, lines_of, span):
        pltpu.make_async_copy(back.at[span, lines_of, mine], home.at[me, span, lines_of], h_sem.at[slot]).start()

        def step(n, carry):
            peer, place = partner(n)
            pltpu.make_async_remote_copy(
                back.at[span, lines_of, pl.ds(pl.multiple_of(peer * 8, 8), 8)], home.at[me, span, lines_of],
                h_out.at[slot], h_sem.at[slot], device_id=place, device_id_type=MESH,
            ).start()
            return carry

        lax.fori_loop(1, 32, step, 0)

    for order, (row, i) in enumerate(lines[:2]):
        whole = recv.at[:, row * 2 + i]
        pltpu.make_async_copy(whole, whole, a_sem.at[order]).wait()
    for share, (begin, size) in enumerate(SHARES):
        span = pl.ds(begin, size)
        arrived = recv.at[span, late]
        pltpu.make_async_copy(arrived, arrived, a_sem.at[2 + share]).wait()

        def solve(n, carry):
            quad = begin + n // 2
            r = 2 * (n % 2)
            field = jnp.concatenate([recv_rows[pl.ds(quad * 1024 + r + odd, 256, stride=4), :] for odd in range(2)], 1)
            full = dot_nn(weight3(wx[0], wx[1]), data3(field, 0))
            factor = jnp.concatenate([green_rows[pl.ds(4 * quad + r + odd, 256, stride=32), :] for odd in range(2)], 1)
            product = jnp.concatenate([full[:256] * factor, full[256:] * factor], 0)
            result = dot_nn(weight3(wxi[0], wxi[1]), data3(product, 0))
            for odd in range(2):
                back_rows[pl.ds(quad * 1024 + r + odd, 256, stride=4), :] = result[:, odd * 128 : odd * 128 + 128]
            return carry

        lax.fori_loop(0, 2 * size, solve, 0)
        give_back(0, pl.ds(other * 2, 2), span)
    for i in range(2):
        give_back(1 + i, pl.ds(yh * 2 + i, 1), pl.ds(0, 8))

    loads[6].wait()

    def inverse_yz(line):
        def step(zt, carry):
            columns = []
            for k in range(2):
                blocks = []
                for c in range(2):
                    for xt in range(4):
                        for r in range(4):
                            start = (xt * 8 + zt * 2 + k) * 256 + line * 8 + c * 4 + r
                            blocks.append(home_rows[pl.ds(start, 8, stride=32), :])
                columns.append(jnp.concatenate(blocks, 0))
            along = dot_nn(weight3(wyi[0], wyi[1]), data3(jnp.concatenate(columns, 1), 0))
            lower = lax.broadcasted_iota(jnp.int32, (128, 128), 1) < 64
            fields = [[], []]
            for k in range(2):
                re, im = [along[c * 128 : c * 128 + 128, k * 128 : k * 128 + 128] for c in range(2)]
                fields[0].append(jnp.where(lower, re, pltpu.roll(im, 64, 1)))
                fields[1].append(jnp.where(lower, pltpu.roll(re, 64, 1), im))
            for e in range(2):
                weight = weight3(wzi[zt * 2 + e, 0], wzi[zt * 2 + e, 1])
                b[zt, e * 256 : e * 256 + 256, :] = dot_nt(weight, data3(jnp.concatenate(fields[e], 1), 1))
            return carry

        lax.fori_loop(0, 4, step, 0)

    def back_to_slabs(i, row):
        for _ in range(1):

            def step(n, carry):
                at = n * 8
                turned = []
                for e in range(2):
                    value = [
                        [b[slots[j], pl.ds(pl.multiple_of(e * 256 + c * 128 + at, 8), 8), :] for c in range(2)]
                        for j in range(4)
                    ]
                    (ar, ai), (br, bi), (cr, ci), (dr, di) = [
                        (value[l][0] + s * value[m][0], value[l][1] + s * value[m][1])
                        for l, m, s in ((0, 2, 1.0), (0, 2, -1.0), (1, 3, 1.0), (1, 3, -1.0))
                    ]
                    sums = [(ar + cr, ai + ci), (br - di, bi + dr), (ar - cr, ai - ci), (br + di, bi - dr)]
                    turned.append(
                        [
                            (re * cos_t[e][k] - im * sin_t[e][k], re * sin_t[e][k] + im * cos_t[e][k])
                            for k, (re, im) in enumerate(sums)
                        ]
                    )
                for k in range(4):
                    part[0, row, i, k, pl.ds(pl.multiple_of(at, 8), 8), :] = turned[0][k][0] + turned[1][k][0]
                    part[1, row, i, k, pl.ds(pl.multiple_of(at, 8), 8), :] = sigma * (turned[0][k][0] - turned[1][k][1])
                return carry

            lax.fori_loop(0, 16, step, 0)

    def sum_copy(i, member):
        slot = ((ym - member) & 3) - 1
        return pltpu.make_async_remote_copy(
            part.at[member >> 1, member & 1, i], partial.at[slot, i], r_out.at[i], r_sem.at[i, slot],
            device_id=ring(member), device_id_type=MESH,
        )

    def home_line(row, i):
        inverse_yz(row * 2 + i)
        back_to_slabs(i, row)

    def finish(i):
        for slot in (0, 1, 2) if i == 0 else (0, 2):
            pltpu.make_async_copy(partial.at[slot, i], partial.at[slot, i], r_sem.at[i, slot]).wait()

        def add(k, carry):
            value = part[yl, yh, i, k] + partial[0, i, k] + partial[2, i, k]
            total[k, i] = value + partial[1, i, k] if i == 0 else value
            return carry

        lax.fori_loop(0, 4, add, 0)
        pltpu.make_async_copy(total.at[z, i, pl.ds(core * 64, 64)], final.at[q, i], f_sem.at[i]).start()

        def return_slab(step, carry):
            peer = (q + step) & 7
            pltpu.make_async_remote_copy(
                total.at[peer >> 1, i, pl.ds((peer & 1) * 64, 64)], final.at[q, i], f_out.at[i], f_sem.at[i],
                device_id=(yl * 8 + peer, ta), device_id_type=MESH,
            ).start()
            return carry

        lax.fori_loop(1, 8, return_slab, 0)

    def return_across(step, carry):
        peer = (q + step) & 7
        pltpu.make_async_remote_copy(
            part.at[1 - yl, yh, 1, peer >> 1, pl.ds((peer & 1) * 64, 64)], extra.at[q], x_out, x_sem,
            device_id=across(peer), device_id_type=MESH,
        ).start()
        return carry

    both = home.at[:, :, pl.ds(other * 2, 2)]
    pltpu.make_async_copy(both, both, h_sem.at[0]).wait()
    for i in range(2):
        home_line(other, i)
        sum_copy(i, other).start()
        sum_copy(i, 2 + other).start()
    for i in range(2):
        single = home.at[:, :, yh * 2 + i]
        pltpu.make_async_copy(single, single, h_sem.at[1 + i]).wait()
        home_line(yh, i)
        if i == 0:
            sum_copy(i, (1 - yl) * 2 + yh).start()
        else:
            lax.fori_loop(0, 8, return_across, 0)
        finish(i)
    out_rows = out.reshape(64 * 16, 128)
    for i in range(2):
        pltpu.make_async_copy(final.at[:, i], final.at[:, i], f_sem.at[i]).wait()
        if i == 1:
            pltpu.make_async_copy(extra, extra, x_sem).wait()
        for n in range(8):
            out_rows[pl.ds(2 * n + i, 64, stride=16), :] = final[n, i] + extra[n] if i else final[n, i]

    def drain(ref, sem):
        pltpu.make_async_copy(ref, ref, sem).wait()

    drain(zs.at[pl.ds(0, 14)], z_out)
    for i in range(2):
        drain(raw.at[pl.ds(0, 3), i], y_out.at[i])
    for order in range(2):
        drain(send.at[pl.ds(0, 31), :, order], a_out.at[order])
    drain(send.at[pl.ds(0, 31), :, pl.ds(0, 2)], a_out.at[2])
    drain(home.at[pl.ds(0, 31), :, pl.ds(0, 2)], h_out.at[0])
    for i in range(2):
        drain(home.at[pl.ds(0, 31), :, i], h_out.at[1 + i])
        drain(partial.at[pl.ds(0, 3 - i), i], r_out.at[i])
        drain(final.at[pl.ds(0, 7), i], f_out.at[i])
    drain(extra, x_out)


def on_device(consts, charge, green_hat):
    any_spec = pl.BlockSpec(memory_space=pl.ANY)
    vmem_spec = pl.BlockSpec(memory_space=pltpu.VMEM)
    dma = pltpu.SemaphoreType.DMA
    return pl.pallas_call(
        kernel,
        out_shape=jax.ShapeDtypeStruct((64, 16, 128), F32),
        in_specs=[vmem_spec] + [any_spec] * 7,
        out_specs=vmem_spec,
        scratch_shapes=[
            pltpu.VMEM((256, 32, 128), F32),
            pltpu.VMEM((2, 512, 256), BF16),
            pltpu.VMEM((2, 256, 512), BF16),
            pltpu.VMEM((2, 256, 256), BF16),
            pltpu.VMEM((2, 256, 256), BF16),
            pltpu.VMEM((2, 128, 128), F32),
            pltpu.VMEM((8, 8, 128), F32),
            pltpu.VMEM((8, 2, 256, 256), BF16),
            pltpu.VMEM((8, 2, 256, 256), BF16),
            pltpu.VMEM((16, 64, 128), F32),
            pltpu.VMEM((4, 2, 4, 128, 128), F32),
            pltpu.VMEM((4, 2, 2, 256, 128), BF16),
            pltpu.VMEM((32, 8, 4, 8, 128), F32),
            pltpu.VMEM((8, 4, 256, 128), F32),
            pltpu.VMEM((8, 4, 256, 128), F32),
            pltpu.VMEM((32, 8, 4, 8, 128), F32),
            pltpu.VMEM((4, 512, 128), F32),
            pltpu.VMEM((2, 2, 2, 4, 128, 128), F32),
            pltpu.VMEM((3, 2, 4, 128, 128), F32),
            pltpu.VMEM((4, 2, 128, 128), F32),
            pltpu.VMEM((8, 2, 64, 128), F32),
            dma((7,)),
            dma((2,)),
            dma,
            dma((2, 3)),
            dma((2,)),
            dma((2 + len(SHARES),)),
            dma((4,)),
            dma((3,)),
            dma((3,)),
            dma((2, 3)),
            dma((2,)),
            dma((2,)),
            dma((2,)),
            pltpu.VMEM((8, 64, 128), F32),
            dma,
            dma,
        ],
        compiler_params=pltpu.CompilerParams(
            collective_id=0, has_side_effects=True, vmem_limit_bytes=60 * 1024 * 1024
        ),
    )(charge, green_hat, *consts)


def solution(mesh):
    consts = tables()
    return jax.shard_map(
        functools.partial(on_device, consts),
        mesh=mesh,
        in_specs=(P("gz", "ta", None), P(None, "ta", "gz")),
        out_specs=P("gz", "ta", None),
        check_vma=False,
    )
```

```python
import functools

import jax
import jax.numpy as jnp
import ml_dtypes
import numpy as np
from jax import lax
from jax.experimental import pallas as pl
from jax.experimental.pallas import tpu as pltpu
from jax.sharding import PartitionSpec as P

MESH = pl.DeviceIdType.MESH
F32 = jnp.float32
BF16 = jnp.bfloat16
SHARES = ((0, 3), (3, 3), (6, 2))


def halves(table):
    high = table.astype(ml_dtypes.bfloat16)
    low = (table - high.astype(np.float64)).astype(ml_dtypes.bfloat16)
    return np.stack([high, low])


def tables():
    peer = np.arange(32)
    row = np.arange(4)
    x_of = ((peer // 8) * 16 + (peer % 8) * 2)[None, :] + ((row // 2) * 64 + row % 2)[:, None]
    kx = np.arange(256)
    angle = 2 * np.pi / 256 * (kx[:, None, None] * x_of[None] % 256)
    cosine, sine = np.cos(angle), np.sin(angle)
    wx = np.stack([np.stack([cosine, sine], 3), np.stack([-sine, cosine], 3)]).reshape(512, 256)
    y = np.arange(128)
    wy = []
    for y_half in range(2):
        ky = 128 * y_half + np.arange(128).reshape(4, 8, 4).transpose(0, 2, 1).reshape(128)
        angle = 2 * np.pi / 256 * (ky[:, None] * y[None] % 256)
        cosine, sine = np.cos(angle), np.sin(angle)
        wy.append(np.block([[cosine, sine], [-sine, cosine]]))
    wy = np.stack(wy)
    v = np.arange(128)
    low_bits = np.concatenate([2 * np.arange(64), 2 * np.arange(64) + 1])
    angle = 2 * np.pi / 128 * (low_bits[:, None] * v[None] % 128)
    alpha = np.stack([np.cos(angle), np.sin(angle)]).astype(np.float32)
    reverse = np.array([0, 2, 1, 3])
    s = 4 * reverse[None, :, None] + 2 * np.arange(2)[:, None, None] + np.arange(2)[None, None]
    angle = 2 * np.pi / 2048 * (s.reshape(2, 8)[..., None] * v % 2048)
    beta = np.stack([np.cos(angle), np.sin(angle)], 2).astype(np.float32)
    beta = np.pad(beta, ((0, 0), (0, 0), (0, 6), (0, 0)))
    return (
        halves(wx),
        halves(wx.T * 2.0**-27),
        np.stack([halves(w) for w in wy]),
        np.stack([halves(w.T) for w in wy]),
        alpha,
        beta,
    )


def split(value):
    high = value.astype(BF16)
    return high, (value - high.astype(F32)).astype(BF16)


def weight3(high, low):
    return jnp.concatenate([high, high, low], axis=1)


def data3(value, axis):
    high, low = split(value)
    return jnp.concatenate([high, low, high], axis=axis)


def dot_nn(weight, data):
    return jnp.dot(weight, data, preferred_element_type=F32)


def dot_nt(weight, data):
    return lax.dot_general(weight, data, (((1,), (1,)), ((), ())), preferred_element_type=F32)


def kernel(
    charge, green, wx_hbm, wxi_hbm, wy_hbm, wyi_hbm, alpha_hbm, beta_hbm,
    out,
    g, wx, wxi, wy, wyi, alpha, beta, wz, wzi, zs, raw, a, send, recv, back, home, b, part, partial, total, final,
    load_sem, z_sem, z_out, y_sem, y_out, a_sem, a_out, h_sem, h_out, r_sem, r_out, f_sem, f_out, extra, x_sem, x_out,
):
    gz = lax.axis_index("gz")
    ta = lax.axis_index("ta")
    yl, q = gz >> 3, gz & 7
    z, core = q >> 1, q & 1
    yh, xc = ta >> 2, ta & 3
    ym = yl * 2 + yh
    me = xc * 8 + q

    def plane(peer):
        return (yl * 8 + (peer & 7), yh * 4 + (peer >> 3))

    def ring(member):
        return ((member >> 1) * 8 + q, (member & 1) * 4 + xc)

    def across(peer):
        return ((1 - yl) * 8 + peer, ta)

    loads = [
        pltpu.make_async_copy(alpha_hbm, alpha, load_sem.at[0]),
        pltpu.make_async_copy(beta_hbm.at[yl], beta, load_sem.at[1]),
        pltpu.make_async_copy(wy_hbm.at[yh], wy, load_sem.at[2]),
        pltpu.make_async_copy(wx_hbm, wx, load_sem.at[3]),
        pltpu.make_async_copy(green, g, load_sem.at[4]),
        pltpu.make_async_copy(wxi_hbm, wxi, load_sem.at[5]),
        pltpu.make_async_copy(wyi_hbm.at[yh], wyi, load_sem.at[6]),
    ]
    for load in loads:
        load.start()

    barrier = pltpu.get_barrier_semaphore()

    def greet(step, carry):
        pl.semaphore_signal(barrier, inc=1, device_id=plane((me + step) & 31), device_id_type=MESH)
        return carry

    lax.fori_loop(1, 32, greet, 0)
    for step in range(1, 4):
        pl.semaphore_signal(barrier, inc=1, device_id=ring((ym + step) & 3), device_id_type=MESH)

    def greet_across(step, carry):
        pl.semaphore_signal(barrier, inc=1, device_id=across((q + step) & 7), device_id_type=MESH)
        return carry

    lax.fori_loop(1, 8, greet_across, 0)
    rows = charge.reshape(64 * 16, 128)
    for x in range(16):
        zs[x] = rows[pl.ds(x, 64, stride=16), :]
    pl.semaphore_wait(barrier, 41)

    for i in range(2):
        keep = pltpu.make_async_copy(
            zs.at[2 * q + i], raw.at[ym, i, z, pl.ds(core * 64, 64)], z_sem.at[i]
        )
        keep.start()

        if i == 0:

            def spread_across(step, carry):
                peer = (q + step) & 7
                pltpu.make_async_remote_copy(
                    zs.at[2 * peer], raw.at[ym, 0, z, pl.ds(core * 64, 64)], y_out.at[0], y_sem.at[0, 1],
                    device_id=across(peer), device_id_type=MESH,
                ).start()
                return carry

            lax.fori_loop(0, 8, spread_across, 0)

        def spread(step, carry):
            peer = (q + step) & 7
            pltpu.make_async_remote_copy(
                zs.at[2 * peer + i], raw.at[ym, i, z, pl.ds(core * 64, 64)], z_out, z_sem.at[i],
                device_id=(yl * 8 + peer, ta), device_id_type=MESH,
            ).start()
            return carry

        lax.fori_loop(1, 8, spread, 0)

    loads[0].wait()
    loads[1].wait()

    def build(slot, carry):
        turn = beta[slot]
        cos_b, sin_b = turn[0:1], turn[1:2]
        cos_a, sin_a = alpha[0], alpha[1]
        cosine = cos_a * cos_b - sin_a * sin_b
        sine = sin_a * cos_b + cos_a * sin_b
        blocks = []
        for k in range(2):
            c_k, s_k = cosine[k * 64 : k * 64 + 64], sine[k * 64 : k * 64 + 64]
            blocks += [jnp.concatenate([c_k, s_k], 1), jnp.concatenate([-s_k, c_k], 1)]
        table = jnp.concatenate(blocks, 0)
        high, low = split(table)
        wz[slot, 0] = high
        wz[slot, 1] = low
        high, low = split(table.T)
        wzi[slot, 0] = high
        wzi[slot, 1] = low
        return carry

    lax.fori_loop(0, 8, build, 0)

    def ring_copy(i, step):
        return pltpu.make_async_remote_copy(
            raw.at[ym, i], raw.at[ym, i], y_out.at[i], y_sem.at[i, step - 1],
            device_id=ring((ym + step) & 3), device_id_type=MESH,
        )

    for i in range(2):
        pltpu.make_async_copy(raw.at[ym, i], raw.at[ym, i], z_sem.at[i]).wait()
        if i == 1:
            ring_copy(i, 2).start()
    for i in range(2):
        for step in (1, 3):
            ring_copy(i, step).start()

    first = yl == 0
    sigma = jnp.where(first, 1.0, -1.0).astype(F32)

    def pick(zero, one):
        return jnp.where(first, np.float32(zero), np.float32(one))

    cos_t = [[pick(np.cos(np.pi * (e) * n / 8), np.cos(np.pi * (2 + e) * n / 8)) for n in range(4)] for e in range(2)]
    sin_t = [[pick(np.sin(np.pi * (e) * n / 8), np.sin(np.pi * (2 + e) * n / 8)) for n in range(4)] for e in range(2)]
    slots = (0, 2, 1, 3)

    def over_slabs(row, i):
        for _ in range(1):

            def step(n, carry):
                at = pl.multiple_of(n * 16, 16)
                near = [raw[row, i, k, pl.ds(at, 16), :] for k in range(4)]
                far = [raw[2 + row, i, k, pl.ds(at, 16), :] for k in range(4)]
                for e in range(2):
                    re, im = [], []
                    for k in range(4):
                        ct, st = cos_t[e][k], sin_t[e][k]
                        if e == 0:
                            u = near[k] + sigma * far[k]
                            re.append(u * ct if k else u)
                            im.append(-(u * st) if k else jnp.zeros_like(u))
                        else:
                            w = sigma * far[k]
                            re.append(near[k] * ct - w * st if k else near[k])
                            im.append(-(near[k] * st + w * ct) if k else -w)
                    ar, ai = re[0] + re[2], im[0] + im[2]
                    br, bi = re[0] - re[2], im[0] - im[2]
                    cr, ci = re[1] + re[3], im[1] + im[3]
                    dr, di = re[1] - re[3], im[1] - im[3]
                    sums = [(ar + cr, ai + ci), (br + di, bi - dr), (ar - cr, ai - ci), (br - di, bi + dr)]
                    for j in range(4):
                        for c in range(2):
                            high, low = split(sums[j][c])
                            spot = pl.ds(pl.multiple_of(c * 128 + at, 16), 16)
                            a[slots[j], e, 0, spot, :] = high
                            a[slots[j], e, 1, spot, :] = low
                return carry

            lax.fori_loop(0, 8, step, 0)

    send_rows = send.reshape(32 * 256, 128)
    home_rows = home.reshape(32 * 256, 128)
    mine = pl.ds(pl.multiple_of(me * 8, 8), 8)

    def partner(step):
        turn = step >> 1
        xt = (xc + turn) & 3
        zc = (((z + (turn >> 2) + turn) & 3) << 1) + ((core + step) & 1)
        return (xt << 3) + zc, (yl * 8 + zc, yh * 4 + xt)

    def send_lines(lines_of, span, out_sem, sem):
        pltpu.make_async_copy(send.at[me, span, lines_of], recv.at[span, lines_of, mine], sem).start()

        def step(n, carry):
            peer, place = partner(n)
            pltpu.make_async_remote_copy(
                send.at[peer, span, lines_of], recv.at[span, lines_of, mine], out_sem, sem,
                device_id=place, device_id_type=MESH,
            ).start()
            return carry

        lax.fori_loop(1, 32, step, 0)

    def forward_zy(order, line):
        def step(n, carry):
            zt = n
            outs = []
            for e in range(2):
                weight = weight3(wz[zt * 2 + e, 0], wz[zt * 2 + e, 1])
                high, low = a[zt, e, 0], a[zt, e, 1]
                outs.append(dot_nn(weight, jnp.concatenate([high, low, high], 0)))
            field = jnp.concatenate(
                [
                    jnp.concatenate([outs[e][k * 128 : k * 128 + 64], outs[e][k * 128 + 64 : k * 128 + 128]], 1)
                    for k in range(2)
                    for e in range(2)
                ],
                0,
            )
            plane_out = dot_nt(weight3(wy[0], wy[1]), data3(field, 1))
            for c in range(2):
                for xt in range(4):
                    for r in range(4):
                        at = c * 128 + xt * 32 + r * 8
                        for k in range(2):
                            start = (xt * 8 + zt * 2 + k) * 256 + line * 8 + c * 4 + r
                            send_rows[pl.ds(start, 8, stride=32), :] = plane_out[at : at + 8, k * 128 : k * 128 + 128]

            return carry

        lax.fori_loop(0, 4, step, 0)
        if order < 2:
            for begin in (0, 4):
                send_lines(pl.ds(line, 1), pl.ds(begin, 4), a_out.at[order], a_sem.at[order])

    loads[2].wait()
    other = 1 - yh
    lines = ((yh, 0), (yh, 1), (other, 0), (other, 1))
    for order, (row, i) in enumerate(lines):
        for step in ((2,) if order < 2 else (1, 3)):
            source = (ym - step) & 3
            pltpu.make_async_copy(raw.at[source, i], raw.at[source, i], y_sem.at[i, step - 1]).wait()
        over_slabs(row, i)
        forward_zy(order, row * 2 + i)

    late = pl.ds(other * 2, 2)
    for share, (begin, size) in enumerate(SHARES):
        send_lines(late, pl.ds(begin, size), a_out.at[2], a_sem.at[2 + share])

    loads[3].wait()
    loads[4].wait()
    loads[5].wait()
    green_rows = g.reshape(256 * 32, 128)
    recv_rows = recv.reshape(8 * 1024, 128)
    back_rows = back.reshape(8 * 1024, 128)

    def give_back(slot, lines_of, span):
        pltpu.make_async_copy(back.at[span, lines_of, mine], home.at[me, span, lines_of], h_sem.at[slot]).start()

        def step(n, carry):
            peer, place = partner(n)
            pltpu.make_async_remote_copy(
                back.at[span, lines_of, pl.ds(pl.multiple_of(peer * 8, 8), 8)], home.at[me, span, lines_of],
                h_out.at[slot], h_sem.at[slot], device_id=place, device_id_type=MESH,
            ).start()
            return carry

        lax.fori_loop(1, 32, step, 0)

    for order, (row, i) in enumerate(lines[:2]):
        whole = recv.at[:, row * 2 + i]
        pltpu.make_async_copy(whole, whole, a_sem.at[order]).wait()
    for share, (begin, size) in enumerate(SHARES):
        span = pl.ds(begin, size)
        arrived = recv.at[span, late]
        pltpu.make_async_copy(arrived, arrived, a_sem.at[2 + share]).wait()

        def solve(n, carry):
            quad = begin + n // 2
            r = 2 * (n % 2)
            field = jnp.concatenate([recv_rows[pl.ds(quad * 1024 + r + odd, 256, stride=4), :] for odd in range(2)], 1)
            full = dot_nn(weight3(wx[0], wx[1]), data3(field, 0))
            factor = jnp.concatenate([green_rows[pl.ds(4 * quad + r + odd, 256, stride=32), :] for odd in range(2)], 1)
            product = jnp.concatenate([full[:256] * factor, full[256:] * factor], 0)
            result = dot_nn(weight3(wxi[0], wxi[1]), data3(product, 0))
            for odd in range(2):
                back_rows[pl.ds(quad * 1024 + r + odd, 256, stride=4), :] = result[:, odd * 128 : odd * 128 + 128]
            return carry

        lax.fori_loop(0, 2 * size, solve, 0)
        give_back(0, pl.ds(other * 2, 2), span)
    for i in range(2):
        give_back(1 + i, pl.ds(yh * 2 + i, 1), pl.ds(0, 8))

    loads[6].wait()

    def inverse_yz(line):
        def step(zt, carry):
            columns = []
            for k in range(2):
                blocks = []
                for c in range(2):
                    for xt in range(4):
                        for r in range(4):
                            start = (xt * 8 + zt * 2 + k) * 256 + line * 8 + c * 4 + r
                            blocks.append(home_rows[pl.ds(start, 8, stride=32), :])
                columns.append(jnp.concatenate(blocks, 0))
            along = dot_nn(weight3(wyi[0], wyi[1]), data3(jnp.concatenate(columns, 1), 0))
            lower = lax.broadcasted_iota(jnp.int32, (128, 128), 1) < 64
            fields = [[], []]
            for k in range(2):
                re, im = [along[c * 128 : c * 128 + 128, k * 128 : k * 128 + 128] for c in range(2)]
                fields[0].append(jnp.where(lower, re, pltpu.roll(im, 64, 1)))
                fields[1].append(jnp.where(lower, pltpu.roll(re, 64, 1), im))
            for e in range(2):
                weight = weight3(wzi[zt * 2 + e, 0], wzi[zt * 2 + e, 1])
                b[zt, e * 256 : e * 256 + 256, :] = dot_nt(weight, data3(jnp.concatenate(fields[e], 1), 1))
            return carry

        lax.fori_loop(0, 4, step, 0)

    def back_to_slabs(i, row):
        for _ in range(1):

            def step(n, carry):
                at = n * 8
                turned = []
                for e in range(2):
                    value = [
                        [b[slots[j], pl.ds(pl.multiple_of(e * 256 + c * 128 + at, 8), 8), :] for c in range(2)]
                        for j in range(4)
                    ]
                    (ar, ai), (br, bi), (cr, ci), (dr, di) = [
                        (value[l][0] + s * value[m][0], value[l][1] + s * value[m][1])
                        for l, m, s in ((0, 2, 1.0), (0, 2, -1.0), (1, 3, 1.0), (1, 3, -1.0))
                    ]
                    sums = [(ar + cr, ai + ci), (br - di, bi + dr), (ar - cr, ai - ci), (br + di, bi - dr)]
                    turned.append(
                        [
                            (re * cos_t[e][k] - im * sin_t[e][k], re * sin_t[e][k] + im * cos_t[e][k])
                            for k, (re, im) in enumerate(sums)
                        ]
                    )
                for k in range(4):
                    part[0, row, i, k, pl.ds(pl.multiple_of(at, 8), 8), :] = turned[0][k][0] + turned[1][k][0]
                    part[1, row, i, k, pl.ds(pl.multiple_of(at, 8), 8), :] = sigma * (turned[0][k][0] - turned[1][k][1])
                return carry

            lax.fori_loop(0, 16, step, 0)

    def sum_copy(i, member):
        slot = ((ym - member) & 3) - 1
        return pltpu.make_async_remote_copy(
            part.at[member >> 1, member & 1, i], partial.at[slot, i], r_out.at[i], r_sem.at[i, slot],
            device_id=ring(member), device_id_type=MESH,
        )

    def home_line(row, i):
        inverse_yz(row * 2 + i)
        back_to_slabs(i, row)

    def finish(i):
        for slot in (0, 1, 2) if i == 0 else (0, 2):
            pltpu.make_async_copy(partial.at[slot, i], partial.at[slot, i], r_sem.at[i, slot]).wait()

        def add(k, carry):
            value = part[yl, yh, i, k] + partial[0, i, k] + partial[2, i, k]
            total[k, i] = value + partial[1, i, k] if i == 0 else value
            return carry

        lax.fori_loop(0, 4, add, 0)
        pltpu.make_async_copy(total.at[z, i, pl.ds(core * 64, 64)], final.at[q, i], f_sem.at[i]).start()

        def return_slab(step, carry):
            peer = (q + step) & 7
            pltpu.make_async_remote_copy(
                total.at[peer >> 1, i, pl.ds((peer & 1) * 64, 64)], final.at[q, i], f_out.at[i], f_sem.at[i],
                device_id=(yl * 8 + peer, ta), device_id_type=MESH,
            ).start()
            return carry

        lax.fori_loop(1, 8, return_slab, 0)

    def return_across(step, carry):
        peer = (q + step) & 7
        pltpu.make_async_remote_copy(
            part.at[1 - yl, yh, 1, peer >> 1, pl.ds((peer & 1) * 64, 64)], extra.at[q], x_out, x_sem,
            device_id=across(peer), device_id_type=MESH,
        ).start()
        return carry

    both = home.at[:, :, pl.ds(other * 2, 2)]
    pltpu.make_async_copy(both, both, h_sem.at[0]).wait()
    for i in range(2):
        home_line(other, i)
        sum_copy(i, other).start()
        sum_copy(i, 2 + other).start()
    for i in range(2):
        single = home.at[:, :, yh * 2 + i]
        pltpu.make_async_copy(single, single, h_sem.at[1 + i]).wait()
        home_line(yh, i)
        if i == 0:
            sum_copy(i, (1 - yl) * 2 + yh).start()
        else:
            lax.fori_loop(0, 8, return_across, 0)
            finish(0)
            finish(1)
    out_rows = out.reshape(64 * 16, 128)
    for i in range(2):
        pltpu.make_async_copy(final.at[:, i], final.at[:, i], f_sem.at[i]).wait()
        if i == 1:
            pltpu.make_async_copy(extra, extra, x_sem).wait()
        for n in range(8):
            out_rows[pl.ds(2 * n + i, 64, stride=16), :] = final[n, i] + extra[n] if i else final[n, i]

    def drain(ref, sem):
        pltpu.make_async_copy(ref, ref, sem).wait()

    drain(zs.at[pl.ds(0, 14)], z_out)
    for i in range(2):
        drain(raw.at[pl.ds(0, 3), i], y_out.at[i])
    for order in range(2):
        drain(send.at[pl.ds(0, 31), :, order], a_out.at[order])
    drain(send.at[pl.ds(0, 31), :, pl.ds(0, 2)], a_out.at[2])
    drain(home.at[pl.ds(0, 31), :, pl.ds(0, 2)], h_out.at[0])
    for i in range(2):
        drain(home.at[pl.ds(0, 31), :, i], h_out.at[1 + i])
        drain(partial.at[pl.ds(0, 3 - i), i], r_out.at[i])
        drain(final.at[pl.ds(0, 7), i], f_out.at[i])
    drain(extra, x_out)


def on_device(consts, charge, green_hat):
    any_spec = pl.BlockSpec(memory_space=pl.ANY)
    vmem_spec = pl.BlockSpec(memory_space=pltpu.VMEM)
    dma = pltpu.SemaphoreType.DMA
    return pl.pallas_call(
        kernel,
        out_shape=jax.ShapeDtypeStruct((64, 16, 128), F32),
        in_specs=[vmem_spec] + [any_spec] * 7,
        out_specs=vmem_spec,
        scratch_shapes=[
            pltpu.VMEM((256, 32, 128), F32),
            pltpu.VMEM((2, 512, 256), BF16),
            pltpu.VMEM((2, 256, 512), BF16),
            pltpu.VMEM((2, 256, 256), BF16),
            pltpu.VMEM((2, 256, 256), BF16),
            pltpu.VMEM((2, 128, 128), F32),
            pltpu.VMEM((8, 8, 128), F32),
            pltpu.VMEM((8, 2, 256, 256), BF16),
            pltpu.VMEM((8, 2, 256, 256), BF16),
            pltpu.VMEM((16, 64, 128), F32),
            pltpu.VMEM((4, 2, 4, 128, 128), F32),
            pltpu.VMEM((4, 2, 2, 256, 128), BF16),
            pltpu.VMEM((32, 8, 4, 8, 128), F32),
            pltpu.VMEM((8, 4, 256, 128), F32),
            pltpu.VMEM((8, 4, 256, 128), F32),
            pltpu.VMEM((32, 8, 4, 8, 128), F32),
            pltpu.VMEM((4, 512, 128), F32),
            pltpu.VMEM((2, 2, 2, 4, 128, 128), F32),
            pltpu.VMEM((3, 2, 4, 128, 128), F32),
            pltpu.VMEM((4, 2, 128, 128), F32),
            pltpu.VMEM((8, 2, 64, 128), F32),
            dma((7,)),
            dma((2,)),
            dma,
            dma((2, 3)),
            dma((2,)),
            dma((2 + len(SHARES),)),
            dma((4,)),
            dma((3,)),
            dma((3,)),
            dma((2, 3)),
            dma((2,)),
            dma((2,)),
            dma((2,)),
            pltpu.VMEM((8, 64, 128), F32),
            dma,
            dma,
        ],
        compiler_params=pltpu.CompilerParams(
            collective_id=0, has_side_effects=True, vmem_limit_bytes=60 * 1024 * 1024
        ),
    )(charge, green_hat, *consts)


def solution(mesh):
    consts = tables()
    return jax.shard_map(
        functools.partial(on_device, consts),
        mesh=mesh,
        in_specs=(P("gz", "ta", None), P(None, "ta", "gz")),
        out_specs=P("gz", "ta", None),
        check_vma=False,
    )
```
